32 devices in a mesh: grp: 16 (over z, x, core), patch: 2 (over y).
Axes of the slice: x: 2, y: 2, z: 4, core: 2. Of those that a mesh axis runs over, the one named last changes fastest.
Arguments:
- tokens: bfloat16 [12288, 1152], P(('grp', 'patch')), parts along dimension 0, may hold values from -6 to 6
- projection_weight: bfloat16 [1152, 3456], replicated, may hold values from -0.1875 to 0.1875
- shift_term: float32 [1152], replicated, may hold values from -3 to 3
- scale_term: float32 [1152], replicated, may hold values from -3 to 3
- query_gain: float32 [72], replicated, may hold values from 0.1 to 1.9
- key_gain: float32 [72], replicated, may hold values from 0.1 to 1.9
- stale_keys: bfloat16 [12288, 1152], P(('grp', 'patch')), parts along dimension 0, may hold values from -6 to 6
- stale_values: bfloat16 [12288, 1152], P(('grp', 'patch')), parts along dimension 0, may hold values from -6 to 6
- stale_output: bfloat16 [12288, 1152], P(('grp', 'patch')), parts along dimension 0, may hold values from -3 to 3
- refreshed: int32 [768], P('grp'), parts along dimension 0, may hold values from 0 to 1, as said below
Outputs:
- attended: bfloat16 [12288, 1152], P(('grp', 'patch')), parts along dimension 0
The draws below stay inside these ranges and needn't reach their ends.
There are 16 independent parts, one for each index of `grp`. The reference program is written for one: setup_inputs(seed, part) draws one part's arguments, and reference() takes and returns one part's arrays. A program takes and returns all parts, laid end to end along the dimension named above; an argument that names none is the same for every part. Nothing has to cross between parts.
Inputs may be any that keep to these rules, and one draw needn't show every extreme that they name: Exactly 16 of the 48 entries are 1; in every prompt some device has all 16 of its tiles refreshed.
All inputs are finite; a program needn't handle non-finite values.
Results may differ from the reference program's by a relative error of at most 0.0045.
Values may be sent and summed in bfloat16 or wider, within the bound.
No kernel may reach another device: no remote copies, remote signals or barrier semaphores. Data moves between devices by JAX's collectives and lax.ppermute only.
A program may use at most 128 MiB of HBM per device.

```python
import math
import jax
import jax.numpy as jnp
from jax import lax

D = 1152
H = 16
HD = 72
TILE = 16
TILES_DEV = 24
TOKENS = 768
TILES = 48
REFRESHED = 16


def draw_refreshed(key, part):
    heavy_key = jax.random.fold_in(key, 11)
    order_key = jax.random.fold_in(key, 12)
    heavy = jax.random.randint(heavy_key, (), 0, TILES // TILES_DEV)
    ordering = jax.random.permutation(order_key, TILES).astype(jnp.int32)
    holder = jnp.arange(TILES, dtype=jnp.int32) // TILES_DEV
    scores = ordering + jnp.where(holder == heavy, TILES, 0).astype(jnp.int32)
    leading = jnp.argsort(-scores, stable=True)[:REFRESHED]
    return jnp.zeros((TILES,), jnp.int32).at[leading].set(1)


def block_levels(own_key, dims, cuts, low, largest):
    factor_of = 1.0
    for dim, shards_of in cuts:
        heights = jax.random.uniform(jax.random.fold_in(jax.random.fold_in(own_key, 6), dim), (shards_of,), jnp.float32, low / len(cuts), largest / len(cuts))
        factor_of = factor_of * jnp.repeat(jnp.exp(heights), dims[dim] // shards_of).reshape((-1,) + (1,) * (len(dims) - 1 - dim))
    return factor_of


def noise(own_key, dims, deviation, most, pieces=(), kind=jnp.bfloat16):
    factor_of = block_levels(own_key, dims, pieces, -0.22, 0.18) if pieces else 1.0
    result = jax.random.normal(own_key, dims, jnp.float32) * deviation * factor_of
    return jnp.minimum(jnp.maximum(result, -most), most).astype(kind)


def setup_inputs(seed: int = 0, part: int = 0) -> dict:
    arg_keys = jax.random.split(jax.random.key(seed), 11)
    part_splits = jax.random.split(jax.random.fold_in(arg_keys[10], part), 11)
    return {
        "tokens": noise(part_splits[0], (TOKENS, D), 1.0, 6.0, ((0, 2),)),
        "projection_weight": noise(arg_keys[1], (D, 3 * D), D ** -0.5, 0.1875),
        "shift_term": noise(arg_keys[2], (D,), 0.5, 3.0, (), jnp.float32),
        "scale_term": noise(arg_keys[3], (D,), 0.5, 3.0, (), jnp.float32),
        "query_gain": jnp.clip(1.0 + 0.18 * jax.random.normal(arg_keys[4], (HD,), jnp.float32), 0.1, 1.9),
        "key_gain": jnp.clip(1.0 + 0.18 * jax.random.normal(arg_keys[5], (HD,), jnp.float32), 0.1, 1.9),
        "stale_keys": noise(part_splits[6], (TOKENS, D), 1.0, 6.0, ((0, 2),)),
        "stale_values": noise(part_splits[7], (TOKENS, D), 1.0, 6.0, ((0, 2),)),
        "stale_output": noise(part_splits[8], (TOKENS, D), 0.5, 3.0, ((0, 2),)),
        "refreshed": draw_refreshed(jax.random.fold_in(jax.random.fold_in(arg_keys[10], part), 71), part),
    }


epsilon = 1e-06

def modulate(row_block, shift_term, scale_term):
    values = row_block.astype(jnp.float32)
    center = values - lax.optimization_barrier(jnp.mean(values, axis=-1, keepdims=True))
    spread = lax.optimization_barrier(jnp.mean(center * center, axis=-1, keepdims=True))
    normed = center / jnp.sqrt(spread + epsilon)
    return (normed * (1.0 + scale_term) + shift_term).astype(jnp.bfloat16)

def head_norm(row_block, gain_vector, head_count):
    values = row_block.astype(jnp.float32).reshape(row_block.shape[0], head_count, -1)
    normed = values / jnp.sqrt(lax.optimization_barrier(jnp.mean(values * values, axis=-1, keepdims=True)) + epsilon)
    return (normed * gain_vector).astype(jnp.bfloat16).reshape(row_block.shape[0], -1)

def reference(tokens, projection_weight, shift_term, scale_term, query_gain, key_gain, stale_keys, stale_values, stale_output, refreshed):
    model_width = tokens.shape[1]
    row_mask = jnp.repeat(refreshed, TILE) > 0
    hidden = modulate(tokens, shift_term, scale_term)
    projected = jnp.dot(hidden, projection_weight, preferred_element_type=jnp.float32)
    query_new = projected[:, :model_width].astype(jnp.bfloat16)
    key_new = projected[:, model_width:2 * model_width].astype(jnp.bfloat16)
    value_new = projected[:, 2 * model_width:].astype(jnp.bfloat16)
    keys_all = jnp.where(row_mask[:, None], key_new, stale_keys)
    values_all = jnp.where(row_mask[:, None], value_new, stale_values)
    key_normed = head_norm(keys_all, key_gain, H)
    query_normed = head_norm(query_new, query_gain, H)
    chosen = jnp.nonzero(row_mask, size=REFRESHED * TILE, fill_value=0)[0].astype(jnp.int32)
    selected = query_normed[chosen]
    factor = 1.0 / math.sqrt(HD)
    query_heads = selected.reshape(-1, H, HD).transpose(1, 0, 2)
    key_heads = key_normed.reshape(-1, H, HD).transpose(1, 0, 2)
    value_heads = values_all.reshape(-1, H, HD).transpose(1, 0, 2)

    def per_head(operands):
        query_one, key_one, value_one = operands
        scores = jnp.dot(query_one.astype(jnp.float32), key_one.astype(jnp.float32).T, precision=lax.Precision.HIGHEST) * factor
        weights = jnp.exp(scores)
        totals = lax.optimization_barrier(jnp.sum(weights, axis=1))
        rounded = lax.optimization_barrier(weights.astype(jnp.bfloat16)).astype(jnp.float32)
        numerator = jnp.dot(rounded, value_one.astype(jnp.float32), precision=lax.Precision.HIGHEST)
        return numerator / totals[:, None]
    fresh_heads = lax.map(per_head, (query_heads, key_heads, value_heads))
    fresh_rows = fresh_heads.transpose(1, 0, 2).reshape(-1, model_width).astype(jnp.bfloat16)
    return stale_output.at[chosen].set(fresh_rows)
```

```python
import functools
import math

import jax
import jax.numpy as jnp
from jax import lax
from jax.experimental import pallas as pl
from jax.experimental.pallas import tpu as pltpu
from jax.sharding import PartitionSpec as P

H = 16
TILE = 16


epsilon = 1e-06


def modulate(row_block, shift_term, scale_term):
    values = row_block.astype(jnp.float32)
    center = values - jnp.mean(values, axis=-1, keepdims=True)
    spread = jnp.mean(center * center, axis=-1, keepdims=True)
    normed = center / jnp.sqrt(spread + epsilon)
    return (normed * (1.0 + scale_term) + shift_term).astype(jnp.bfloat16)


def head_norm(row_block, gain_vector, head_count):
    values = row_block.astype(jnp.float32).reshape(row_block.shape[0], head_count, -1)
    normed = values / jnp.sqrt(jnp.mean(values * values, axis=-1, keepdims=True) + epsilon)
    return (normed * gain_vector).astype(jnp.bfloat16).reshape(row_block.shape[0], -1)


def block_size(row_total, row_unit):
    multiple = row_total // row_unit
    chosen = 1
    for candidate in range(1, multiple + 1):
        if multiple % candidate == 0 and candidate * row_unit <= 1024:
            chosen = candidate
    return chosen * row_unit


def partial_terms(queries, key_rows, values, head_count):
    query_count = queries.shape[0]
    model_width = queries.shape[1]
    head_size = model_width // head_count
    factor = 1.0 / math.sqrt(head_size)
    query_heads = queries.reshape(query_count, head_count, head_size)
    key_heads = key_rows.reshape(key_rows.shape[0], head_count, head_size)
    value_heads = values.reshape(values.shape[0], head_count, head_size)
    scores = (
        jnp.einsum("qhd,khd->hqk", query_heads, key_heads, preferred_element_type=jnp.float32)
        * factor
    )
    weights = jnp.exp(scores)
    totals = jnp.sum(weights, axis=2).T
    numerator = jnp.einsum(
        "hqk,khd->qhd",
        weights.astype(jnp.bfloat16),
        value_heads,
        preferred_element_type=jnp.float32,
    )
    return (numerator.reshape(query_count, model_width), totals)


def own_terms(every_query, key_rows, values, head_count, row_unit):
    row_total = every_query.shape[0]
    stride = block_size(row_total, row_unit)

    def advance(turn_index, inner_sums):
        offset = turn_index * stride
        query_block = lax.dynamic_slice_in_dim(every_query, offset, stride, 0)
        numerator, totals = partial_terms(query_block, key_rows, values, head_count)
        return (
            lax.dynamic_update_slice_in_dim(inner_sums[0], numerator, offset, 0),
            lax.dynamic_update_slice_in_dim(inner_sums[1], totals, offset, 0),
        )

    starting = (
        jnp.zeros((row_total, key_rows.shape[1]), jnp.float32),
        jnp.zeros((row_total, head_count), jnp.float32),
    )
    return lax.fori_loop(0, row_total // stride, advance, starting)


def attend(queries, own_keys, own_values, head_count):
    query_count = queries.shape[0]
    model_width = queries.shape[1]
    every_query = lax.all_gather(queries, "patch", axis=0, tiled=True)
    numerator, totals = own_terms(every_query, own_keys, own_values, head_count, query_count)
    numerator, totals = (
        lax.psum_scatter(
            numerator.astype(jnp.bfloat16), "patch", scatter_dimension=0, tiled=True
        ).astype(jnp.float32),
        lax.psum_scatter(
            totals.astype(jnp.bfloat16), "patch", scatter_dimension=0, tiled=True
        ).astype(jnp.float32),
    )
    fresh_heads = numerator.reshape(query_count, head_count, -1) / totals[:, :, None]
    return fresh_heads.reshape(query_count, model_width).astype(jnp.bfloat16)


def body(
    tokens,
    projection_weight,
    shift_term,
    scale_term,
    query_gain,
    key_gain,
    stale_keys,
    stale_values,
    stale_output,
    refreshed,
):
    model_width = tokens.shape[1]
    head_count = H
    own_rows = tokens.shape[0]
    own_tiles = own_rows // TILE
    patch_count = lax.axis_size("patch")
    my_index = lax.axis_index("patch")
    share_tiles = own_tiles // 3
    most_tiles = min(own_tiles, share_tiles * patch_count)
    tile_grid = refreshed.reshape(patch_count, own_tiles)
    my_tiles = lax.dynamic_index_in_dim(tile_grid, my_index, 0, keepdims=False)
    picked = jnp.nonzero(my_tiles, size=most_tiles, fill_value=0)[0].astype(jnp.int32)
    token_tiles = tokens.reshape(own_tiles, TILE, model_width)
    chosen = token_tiles[picked].reshape(most_tiles * TILE, model_width)
    hidden = modulate(chosen, shift_term, scale_term)
    projected = jnp.dot(hidden, projection_weight, preferred_element_type=jnp.float32)
    query_new = projected[:, :model_width].astype(jnp.bfloat16)
    key_new = (
        projected[:, model_width : 2 * model_width]
        .astype(jnp.bfloat16)
        .reshape(most_tiles, TILE, model_width)
    )
    value_new = (
        projected[:, 2 * model_width :].astype(jnp.bfloat16).reshape(most_tiles, TILE, model_width)
    )
    position = jnp.maximum(jnp.cumsum(my_tiles) - 1, 0)
    fresh_tile = (my_tiles > 0)[:, None, None]
    keys_all = jnp.where(
        fresh_tile, key_new[position], stale_keys.reshape(own_tiles, TILE, model_width)
    ).reshape(own_rows, model_width)
    values_all = jnp.where(
        fresh_tile, value_new[position], stale_values.reshape(own_tiles, TILE, model_width)
    ).reshape(own_rows, model_width)
    own_keys = head_norm(keys_all, key_gain, head_count)
    queries = head_norm(query_new, query_gain, head_count)
    fresh_rows = attend(queries, own_keys, values_all, head_count)
    fresh_tiles = fresh_rows.reshape(most_tiles, TILE, model_width)
    merged = jnp.where(
        fresh_tile, fresh_tiles[position], stale_output.reshape(own_tiles, TILE, model_width)
    )
    return merged.reshape(own_rows, model_width)


LANES = 128


def ceil_to(amount, unit):
    return -(-amount // unit) * unit


def lane_window(start, stop):
    return start // LANES * LANES, ceil_to(stop, LANES)


def pair_plan(head_count, own_rows, fresh_rows, chunks):
    ratio = 2 * own_rows // fresh_rows
    shipped = head_count // (1 + ratio)
    asked = head_count - shipped
    if shipped % (2 * chunks) or asked % (2 * chunks):
        return None
    if asked * fresh_rows != shipped * 2 * own_rows:
        return None
    if own_rows % LANES or fresh_rows % LANES:
        return None
    a, s = asked // chunks, shipped // chunks
    return [
        (
            tuple(range(c * a, (c + 1) * a)),
            tuple(range(asked + c * s, asked + (c + 1) * s)),
        )
        for c in range(chunks)
    ]


def pair_body(
    plan,
    tokens,
    projection_weight,
    shift_term,
    scale_term,
    query_gain,
    key_gain,
    stale_keys,
    stale_values,
    stale_output,
    refreshed,
):
    N, D = tokens.shape
    HD = query_gain.shape[0]
    heads = D // HD
    tiles = N // TILE
    patch_count = lax.axis_size("patch")
    R = tiles * patch_count // 3 * TILE
    HP = ceil_to(HD + 1, 16)
    f32, bf16 = jnp.float32, jnp.bfloat16
    factor = math.log2(math.e) / math.sqrt(HD)
    asked = [h for qs, _ in plan for h in qs]
    shipped = [h for _, ks in plan for h in ks]
    hq, hk = len(plan[0][0]), len(plan[0][1])
    qrows, krows = hq * HD, 2 * hk * HD
    xrows = qrows * (R // LANES)
    trows = ceil_to(hq, 8)
    rrows = xrows + ceil_to(2 * trows * (R // LANES), 16)
    VM = pl.BlockSpec(memory_space=pltpu.VMEM)
    ANY = pl.BlockSpec(memory_space=pl.ANY)
    SM = pl.BlockSpec(memory_space=pltpu.SMEM)
    params = pltpu.CompilerParams()
    DMA = pltpu.SemaphoreType.DMA
    vm = pltpu.VMEM

    def sds(rows, cols, dtype):
        return jax.ShapeDtypeStruct((rows, cols), dtype)

    def is_fresh(flags):
        base = lax.axis_index("patch") * tiles
        return lax.fori_loop(0, tiles, lambda t, s: s + flags[base + t], 0) > 0

    def each_tile(flags, action):
        base = lax.axis_index("patch") * tiles

        def step(t, seen):
            flag = flags[base + t]

            @pl.when(flag > 0)
            def _():
                action(pl.multiple_of(t * TILE, TILE), pl.multiple_of(seen * TILE, TILE))

            return seen + flag

        lax.fori_loop(0, tiles, step, 0)

    def column(gain):
        row = jnp.broadcast_to(gain[...].reshape(1, HD), (HD, HD))
        eye = lax.broadcasted_iota(jnp.int32, (HD, HD), 0) == lax.broadcasted_iota(
            jnp.int32, (HD, HD), 1
        )
        return jnp.sum(jnp.where(eye, row, 0.0), axis=1, keepdims=True)

    def turn(source, width, target):
        for j in range(width // LANES):
            target[LANES * j : LANES * (j + 1), :] = source[:, LANES * j : LANES * (j + 1)].astype(f32).T

    def normed(part, gain):
        spread = jnp.mean(part * part, axis=0, keepdims=True)
        return part * lax.rsqrt(spread + epsilon) * gain

    def padded(part, fill):
        extra = jnp.full((HP - HD, part.shape[1]), fill, f32)
        return jnp.concatenate([part, extra], axis=0).astype(bf16)

    def put(target, row, stride, value):
        for b in range(value.shape[1] // LANES):
            target[stride * b + row : stride * b + row + value.shape[0], :] = value[
                :, LANES * b : LANES * (b + 1)
            ]

    def take(source, row, stride, count, width):
        return jnp.concatenate(
            [source[stride * b + row : stride * b + row + count, :] for b in range(width // LANES)],
            axis=1,
        ).astype(f32)

    def pack_queries(projected_turned, low, qs, gain, target):
        for i in range(0, len(qs), 2):
            two = [
                normed(projected_turned[HD * h - low : HD * (h + 1) - low, :], gain)
                for h in qs[i : i + 2]
            ]
            put(target, HD * i, qrows, jnp.concatenate(two, axis=0).astype(bf16))

    def pack_shipped(kbuf, vbuf, turned, low, ks, gain, target):
        width = kbuf.shape[1]
        turn(kbuf, width, turned)
        for i in range(0, len(ks), 2):
            two = [normed(turned[HD * h - low : HD * (h + 1) - low, :], gain) for h in ks[i : i + 2]]
            put(target, HD * i, krows, jnp.concatenate(two, axis=0).astype(bf16))
        turn(vbuf, width, turned)
        for i in range(0, len(ks), 2):
            two = [turned[HD * h - low : HD * (h + 1) - low, :] for h in ks[i : i + 2]]
            put(target, HD * (len(ks) + i), krows, jnp.concatenate(two, axis=0).astype(bf16))

    def score(queries, keys, values):
        scores = lax.dot_general(
            keys, queries, (((0,), (0,)), ((), ())), preferred_element_type=f32
        )
        weights = jnp.exp2(scores * factor).astype(bf16)
        return jnp.dot(values, weights, preferred_element_type=f32)

    qlow0, qhigh0 = lane_window(HD * plan[0][0][0], HD * (plan[0][0][-1] + 1))
    qlow1, qhigh1 = lane_window(HD * (hq if len(plan) > 1 else shipped[0]), D)
    swindow = [lane_window(HD * ks[0], HD * (ks[-1] + 1)) for _, ks in plan]
    swidth = max(b - a for a, b in swindow)

    def front(flags, tok, w, shift, scale, gq, gk, sk, sv, x0, hid, xbuf, wbuf, qt, kbuf, vbuf, st, sems):
        fresh = is_fresh(flags)

        @pl.when(fresh)
        def _():
            wcopy = pltpu.make_async_copy(w.at[:, qlow0:qhigh0], wbuf, sems.at[0])
            each_tile(
                flags,
                lambda t, s: pltpu.make_async_copy(
                    tok.at[pl.ds(t, TILE), :], xbuf.at[pl.ds(s, TILE), :], sems.at[1]
                ).start(),
            )
            wcopy.start()
            pltpu.make_async_copy(tok.at[0:R, :], xbuf, sems.at[1]).wait()
            up = 1.0 + scale[...].reshape(1, D)
            down = shift[...].reshape(1, D)
            for i in range(0, R, 64):
                x = xbuf[i : i + 64, :].astype(f32)
                center = x - jnp.mean(x, axis=1, keepdims=True)
                spread = jnp.mean(center * center, axis=1, keepdims=True)
                hid[i : i + 64, :] = (center * lax.rsqrt(spread + epsilon) * up + down).astype(bf16)
            wcopy.wait()
            projected = jnp.dot(hid[...], wbuf[...], preferred_element_type=f32).astype(bf16)
            turn(projected, qhigh0 - qlow0, qt)
            pack_queries(qt, qlow0, plan[0][0], column(gq), x0)

        @pl.when(jnp.logical_not(fresh))
        def _():
            low, high = swindow[0]
            kcopy = pltpu.make_async_copy(sk.at[:, low:high], kbuf, sems.at[0])
            vcopy = pltpu.make_async_copy(sv.at[:, low:high], vbuf, sems.at[1])
            kcopy.start()
            vcopy.start()
            kcopy.wait()
            vcopy.wait()
            pack_shipped(kbuf, vbuf, st, low, plan[0][1], column(gk), x0)

    width0 = swindow[0][1] - swindow[0][0]
    x0, hidden = pl.pallas_call(
        front,
        out_shape=(sds(xrows, LANES, bf16), sds(R, D, bf16)),
        in_specs=[SM, ANY, ANY, VM, VM, VM, VM, ANY, ANY],
        out_specs=(VM, VM),
        scratch_shapes=[
            vm((R, D), bf16),
            vm((D, qhigh0 - qlow0), bf16),
            vm((qhigh0 - qlow0, R), f32),
            vm((N, width0), bf16),
            vm((N, width0), bf16),
            vm((width0, N), f32),
            DMA((2,)),
        ],
        compiler_params=params,
        name="front",
    )(refreshed, tokens, projection_weight, shift_term, scale_term, query_gain, key_gain, stale_keys, stale_values)

    swap = [(0, 1), (1, 0)]
    sent = [x0]
    got = [lax.ppermute(x0, "patch", swap)]

    more = len(plan) > 1

    def second(flags, hid, w, gq, gk, sk, sv, *rest):
        x1 = rest[0] if more else None
        qx, wbuf, qt, kbuf, vbuf, st, sems = rest[1:] if more else rest
        fresh = is_fresh(flags)

        @pl.when(fresh)
        def _():
            wcopy = pltpu.make_async_copy(w.at[:, qlow1:qhigh1], wbuf, sems.at[0])
            wcopy.start()
            wcopy.wait()
            projected = jnp.dot(hid[...], wbuf[...], preferred_element_type=f32).astype(bf16)
            turn(projected, qhigh1 - qlow1, qt)
            gain = column(gq)
            if more:
                pack_queries(qt, qlow1, plan[1][0], gain, x1)
            for i, h in enumerate(shipped):
                part = normed(qt[HD * h - qlow1 : HD * (h + 1) - qlow1, :], gain)
                qx[HP * i : HP * (i + 1), :] = padded(part, 0.0)

        if more:

            @pl.when(jnp.logical_not(fresh))
            def _():
                low, high = swindow[1]
                kcopy = pltpu.make_async_copy(sk.at[:, low:high], kbuf, sems.at[0])
                vcopy = pltpu.make_async_copy(sv.at[:, low:high], vbuf, sems.at[1])
                kcopy.start()
                vcopy.start()
                kcopy.wait()
                vcopy.wait()
                pack_shipped(kbuf, vbuf, st, low, plan[1][1], column(gk), x1)

    width1 = swindow[-1][1] - swindow[-1][0]
    outs = [sds(len(shipped) * HP, R, bf16)]
    if more:
        outs = [sds(xrows, LANES, bf16)] + outs
    outs = pl.pallas_call(
        second,
        out_shape=tuple(outs),
        in_specs=[SM, VM, ANY, VM, VM, ANY, ANY],
        out_specs=(VM,) * len(outs),
        scratch_shapes=[
            vm((D, qhigh1 - qlow1), bf16),
            vm((qhigh1 - qlow1, R), f32),
            vm((N, width1), bf16),
            vm((N, width1), bf16),
            vm((width1, N), f32),
            DMA((2,)),
        ],
        compiler_params=params,
        name="second",
    )(refreshed, hidden, projection_weight, query_gain, key_gain, stale_keys, stale_values)
    if more:
        sent.append(outs[0])
        got.append(lax.ppermute(outs[0], "patch", swap))
    qx = outs[-1]

    def third(flags, hid, w, gk, sk, sv, so, kt, vt, out, kall, vall, new, wk, wv, turned, sems):
        fresh = is_fresh(flags)
        ocopy = pltpu.make_async_copy(so, out, sems.at[0])
        kcopy = pltpu.make_async_copy(sk, kall, sems.at[1])
        vcopy = pltpu.make_async_copy(sv, vall, sems.at[2])
        kcopy.start()
        vcopy.start()

        @pl.when(fresh)
        def _():
            wkcopy = pltpu.make_async_copy(w.at[:, D : 2 * D], wk, sems.at[3])
            wvcopy = pltpu.make_async_copy(w.at[:, 2 * D : 3 * D], wv, sems.at[4])
            wkcopy.start()
            wvcopy.start()
            kcopy.wait()
            wkcopy.wait()
            new[...] = jnp.dot(hid[...], wk[...], preferred_element_type=f32).astype(bf16)

            def merge_keys(t, s):
                kall[pl.ds(t, TILE), :] = new[pl.ds(s, TILE), :]

            each_tile(flags, merge_keys)
            vcopy.wait()
            wvcopy.wait()
            new[...] = jnp.dot(hid[...], wv[...], preferred_element_type=f32).astype(bf16)

            def merge_values(t, s):
                vall[pl.ds(t, TILE), :] = new[pl.ds(s, TILE), :]

            each_tile(flags, merge_values)

        @pl.when(jnp.logical_not(fresh))
        def _():
            kcopy.wait()
            vcopy.wait()

        ocopy.start()
        gain = column(gk)
        turn(kall, D, turned)
        for h in range(heads):
            kt[HP * h : HP * (h + 1), :] = padded(normed(turned[HD * h : HD * (h + 1), :], gain), 0.0)
        turn(vall, D, turned)
        for h in range(heads):
            vt[HP * h : HP * (h + 1), :] = padded(turned[HD * h : HD * (h + 1), :], 1.0)
        ocopy.wait()

    kt, vt, held = pl.pallas_call(
        third,
        out_shape=(sds(heads * HP, N, bf16), sds(heads * HP, N, bf16), sds(N, D, bf16)),
        in_specs=[SM, VM, ANY, VM, ANY, ANY, ANY],
        out_specs=(VM, VM, ANY),
        scratch_shapes=[
            vm((N, D), bf16),
            vm((N, D), bf16),
            vm((R, D), bf16),
            vm((D, D), bf16),
            vm((D, D), bf16),
            vm((D, N), f32),
            DMA((5,)),
        ],
        compiler_params=params,
        name="third",
    )(refreshed, hidden, projection_weight, key_gain, stale_keys, stale_values, stale_output)

    def query_pair(x, i):
        two = take(x, HD * i, qrows, 2 * HD, R)
        return [padded(two[:HD], 0.0), padded(two[HD:], 0.0)]

    def keys_of(kt, h):
        return kt[HP * h : HP * (h + 1), :]

    def answer(x, kt, vt, qs, target):
        totals = []
        for i in range(0, hq, 2):
            both = []
            for q, h in zip(query_pair(x, i), qs[i : i + 2]):
                terms = score(q, keys_of(kt, h), keys_of(vt, h))
                both.append(terms[:HD])
                totals.append(terms[HD : HD + 1])
            put(target, HD * i, qrows, jnp.concatenate(both, axis=0).astype(bf16))
        if trows > hq:
            totals.append(jnp.zeros((trows - hq, R), f32))
        total = jnp.concatenate(totals, axis=0)
        high = total.astype(bf16)
        low = (total - high.astype(f32)).astype(bf16)
        pieces = [
            piece[:, LANES * b : LANES * (b + 1)].astype(f32)
            for piece in (high, low)
            for b in range(R // LANES)
        ]
        spare = rrows - xrows - len(pieces) * trows
        if spare:
            pieces.append(jnp.zeros((spare, LANES), f32))
        target[xrows:, :] = jnp.concatenate(pieces, axis=0).astype(bf16)

    def own_terms_of(x, kt, vt, qs, target):
        for i in range(0, hq, 2):
            for k, (q, h) in enumerate(zip(query_pair(x, i), qs[i : i + 2])):
                target[HP * (i + k) : HP * (i + k + 1), :] = score(q, keys_of(kt, h), keys_of(vt, h))

    answers, own = [], []
    for c, (qs, _) in enumerate(plan):

        def reply(flags, xr, kt, vt, *rest, c=c, qs=qs):
            fresh = is_fresh(flags)
            if c:
                xs, r, mine = rest
            else:
                (r,) = rest

            @pl.when(jnp.logical_not(fresh))
            def _():
                answer(xr, kt, vt, qs, r)

            if c:

                @pl.when(fresh)
                def _():
                    own_terms_of(xs, kt, vt, plan[c - 1][0], mine)

        extra = [sent[c - 1]] if c else []
        res = pl.pallas_call(
            reply,
            out_shape=(sds(rrows, LANES, bf16),) + ((sds(hq * HP, R, f32),) if c else ()),
            in_specs=[SM, VM, VM, VM] + [VM] * len(extra),
            out_specs=(VM,) * (1 + len(extra)),
            compiler_params=params,
            name="reply",
        )(refreshed, got[c], kt, vt, *extra)
        answers.append(lax.ppermute(res[0], "patch", swap))
        if c:
            own.append(res[1])

    def rest_of(flags, xs, kt, vt, qx, *rest):
        xr = rest[: len(plan)]
        mine, full = rest[len(plan) :]

        @pl.when(is_fresh(flags))
        def _():
            own_terms_of(xs, kt, vt, plan[-1][0], mine)
            for c, (_, ks) in enumerate(plan):
                for i in range(0, hk, 2):
                    ktwo = take(xr[c], HD * i, krows, 2 * HD, N)
                    vtwo = take(xr[c], HD * (hk + i), krows, 2 * HD, N)
                    for k in range(2):
                        h = ks[i + k]
                        at = shipped.index(h)
                        q = qx[HP * at : HP * (at + 1), :]
                        terms = score(q, keys_of(kt, h), keys_of(vt, h)) + score(
                            q,
                            padded(ktwo[HD * k : HD * (k + 1)], 0.0),
                            padded(vtwo[HD * k : HD * (k + 1)], 1.0),
                        )
                        full[HD * at : HD * (at + 1), :] = terms[:HD] / terms[HD : HD + 1]

    mine, full = pl.pallas_call(
        rest_of,
        out_shape=(sds(hq * HP, R, f32), sds(len(shipped) * HD, R, f32)),
        in_specs=[SM, VM, VM, VM, VM] + [VM] * len(plan),
        out_specs=(VM, VM),
        compiler_params=params,
        name="rest",
    )(refreshed, sent[-1], kt, vt, qx, *got)
    own.append(mine)

    def last(flags, full, *rest):
        mine = rest[: len(plan)]
        theirs = rest[len(plan) : 2 * len(plan)]
        _, out, turned, rows, sem = rest[2 * len(plan) :]

        @pl.when(is_fresh(flags))
        def _():
            turned[HD * shipped[0] :, :] = full[...]
            blocks = R // LANES
            for c, (qs, _) in enumerate(plan):
                tail = theirs[c][xrows:, :].astype(f32)
                parts = [tail[trows * k : trows * (k + 1)] for k in range(2 * blocks)]
                total = jnp.concatenate(
                    [parts[b] + parts[blocks + b] for b in range(blocks)], axis=1
                )
                for i in range(0, hq, 2):
                    two = take(theirs[c], HD * i, qrows, 2 * HD, R)
                    for k in range(2):
                        h = i + k
                        terms = mine[c][HP * h : HP * (h + 1), :]
                        top = terms[:HD] + two[HD * k : HD * (k + 1)]
                        bottom = terms[HD : HD + 1] + total[h : h + 1]
                        turned[HD * qs[h] : HD * (qs[h] + 1), :] = top / bottom
            for j in range(D // LANES):
                rows[:, LANES * j : LANES * (j + 1)] = turned[LANES * j : LANES * (j + 1), :].T.astype(bf16)
            each_tile(
                flags,
                lambda t, s: pltpu.make_async_copy(
                    rows.at[pl.ds(s, TILE), :], out.at[pl.ds(t, TILE), :], sem
                ).start(),
            )
            pltpu.make_async_copy(rows, out.at[0:R, :], sem).wait()

    operands = (refreshed, full, *own, *answers, held)
    return pl.pallas_call(
        last,
        out_shape=sds(N, D, bf16),
        in_specs=[SM] + [VM] * (1 + 2 * len(plan)) + [ANY],
        out_specs=ANY,
        input_output_aliases={len(operands) - 1: 0},
        scratch_shapes=[vm((D, R), f32), vm((R, D), bf16), DMA],
        compiler_params=params,
        name="last",
    )(*operands)


def pick_plan(mesh, tokens_shape, width):
    patch = mesh.shape["patch"]
    own_rows = tokens_shape // (mesh.shape["grp"] * patch)
    own_tiles = own_rows // TILE
    fresh_tiles = own_tiles * patch // 3
    if patch != 2 or fresh_tiles > own_tiles:
        return None
    return pair_plan(H, own_rows, fresh_tiles * TILE, CHUNKS)


CHUNKS = 2


def solution(mesh):
    in_specs = (
        P(("grp", "patch"), None),
        P(),
        P(),
        P(),
        P(),
        P(),
        P(("grp", "patch"), None),
        P(("grp", "patch"), None),
        P(("grp", "patch"), None),
        P("grp"),
    )
    out_specs = P(("grp", "patch"), None)

    def whole(*arrays):
        plan = pick_plan(mesh, arrays[0].shape[0], arrays[0].shape[1])
        inner = body if plan is None else functools.partial(pair_body, plan)
        return jax.shard_map(
            inner, mesh=mesh, in_specs=in_specs, out_specs=out_specs, check_vma=False
        )(*arrays)

    return whole
```

```python
import math

import jax
import jax.numpy as jnp
from jax import lax
from jax.experimental import pallas as pl
from jax.experimental.pallas import tpu as pltpu
from jax.sharding import PartitionSpec as P


H = 16
TILE = 16


epsilon = 1e-06


def modulate(row_block, shift_term, scale_term):
    values = row_block.astype(jnp.float32)
    center = values - jnp.mean(values, axis=-1, keepdims=True)
    spread = jnp.mean(center * center, axis=-1, keepdims=True)
    normed = center / jnp.sqrt(spread + epsilon)
    return (normed * (1.0 + scale_term) + shift_term).astype(jnp.bfloat16)


def head_norm(row_block, gain_vector, head_count):
    values = row_block.astype(jnp.float32).reshape(row_block.shape[0], head_count, -1)
    normed = values / jnp.sqrt(jnp.mean(values * values, axis=-1, keepdims=True) + epsilon)
    return (normed * gain_vector).astype(jnp.bfloat16).reshape(row_block.shape[0], -1)


def block_size(row_total, row_unit):
    multiple = row_total // row_unit
    chosen = 1
    for candidate in range(1, multiple + 1):
        if multiple % candidate == 0 and candidate * row_unit <= 1024:
            chosen = candidate
    return chosen * row_unit


def partial_terms(queries, key_rows, values, head_count):
    query_count = queries.shape[0]
    model_width = queries.shape[1]
    head_size = model_width // head_count
    factor = 1.0 / math.sqrt(head_size)
    query_heads = queries.reshape(query_count, head_count, head_size)
    key_heads = key_rows.reshape(key_rows.shape[0], head_count, head_size)
    value_heads = values.reshape(values.shape[0], head_count, head_size)
    scores = (
        jnp.einsum("qhd,khd->hqk", query_heads, key_heads, preferred_element_type=jnp.float32)
        * factor
    )
    weights = jnp.exp(scores)
    totals = jnp.sum(weights, axis=2).T
    numerator = jnp.einsum(
        "hqk,khd->qhd",
        weights.astype(jnp.bfloat16),
        value_heads,
        preferred_element_type=jnp.float32,
    )
    return (numerator.reshape(query_count, model_width), totals)


def own_terms(every_query, key_rows, values, head_count, row_unit):
    row_total = every_query.shape[0]
    stride = block_size(row_total, row_unit)

    def advance(turn_index, inner_sums):
        offset = turn_index * stride
        query_block = lax.dynamic_slice_in_dim(every_query, offset, stride, 0)
        numerator, totals = partial_terms(query_block, key_rows, values, head_count)
        return (
            lax.dynamic_update_slice_in_dim(inner_sums[0], numerator, offset, 0),
            lax.dynamic_update_slice_in_dim(inner_sums[1], totals, offset, 0),
        )

    starting = (
        jnp.zeros((row_total, key_rows.shape[1]), jnp.float32),
        jnp.zeros((row_total, head_count), jnp.float32),
    )
    return lax.fori_loop(0, row_total // stride, advance, starting)


def attend(queries, own_keys, own_values, head_count):
    query_count = queries.shape[0]
    model_width = queries.shape[1]
    every_query = lax.all_gather(queries, "patch", axis=0, tiled=True)
    numerator, totals = own_terms(every_query, own_keys, own_values, head_count, query_count)
    numerator, totals = (
        lax.psum_scatter(
            numerator.astype(jnp.bfloat16), "patch", scatter_dimension=0, tiled=True
        ).astype(jnp.float32),
        lax.psum_scatter(
            totals.astype(jnp.bfloat16), "patch", scatter_dimension=0, tiled=True
        ).astype(jnp.float32),
    )
    fresh_heads = numerator.reshape(query_count, head_count, -1) / totals[:, :, None]
    return fresh_heads.reshape(query_count, model_width).astype(jnp.bfloat16)


def body(
    tokens,
    projection_weight,
    shift_term,
    scale_term,
    query_gain,
    key_gain,
    stale_keys,
    stale_values,
    stale_output,
    refreshed,
):
    model_width = tokens.shape[1]
    head_count = H
    own_rows = tokens.shape[0]
    own_tiles = own_rows // TILE
    patch_count = lax.axis_size("patch")
    my_index = lax.axis_index("patch")
    share_tiles = own_tiles // 3
    most_tiles = min(own_tiles, share_tiles * patch_count)
    tile_grid = refreshed.reshape(patch_count, own_tiles)
    my_tiles = lax.dynamic_index_in_dim(tile_grid, my_index, 0, keepdims=False)
    picked = jnp.nonzero(my_tiles, size=most_tiles, fill_value=0)[0].astype(jnp.int32)
    token_tiles = tokens.reshape(own_tiles, TILE, model_width)
    chosen = token_tiles[picked].reshape(most_tiles * TILE, model_width)
    hidden = modulate(chosen, shift_term, scale_term)
    projected = jnp.dot(hidden, projection_weight, preferred_element_type=jnp.float32)
    query_new = projected[:, :model_width].astype(jnp.bfloat16)
    key_new = (
        projected[:, model_width : 2 * model_width]
        .astype(jnp.bfloat16)
        .reshape(most_tiles, TILE, model_width)
    )
    value_new = (
        projected[:, 2 * model_width :].astype(jnp.bfloat16).reshape(most_tiles, TILE, model_width)
    )
    position = jnp.maximum(jnp.cumsum(my_tiles) - 1, 0)
    fresh_tile = (my_tiles > 0)[:, None, None]
    keys_all = jnp.where(
        fresh_tile, key_new[position], stale_keys.reshape(own_tiles, TILE, model_width)
    ).reshape(own_rows, model_width)
    values_all = jnp.where(
        fresh_tile, value_new[position], stale_values.reshape(own_tiles, TILE, model_width)
    ).reshape(own_rows, model_width)
    own_keys = head_norm(keys_all, key_gain, head_count)
    queries = head_norm(query_new, query_gain, head_count)
    fresh_rows = attend(queries, own_keys, values_all, head_count)
    fresh_tiles = fresh_rows.reshape(most_tiles, TILE, model_width)
    merged = jnp.where(
        fresh_tile, fresh_tiles[position], stale_output.reshape(own_tiles, TILE, model_width)
    )
    return merged.reshape(own_rows, model_width)


LANES = 128


def ceil_to(amount, unit):
    return -(-amount // unit) * unit


def lane_window(start, stop):
    return start // LANES * LANES, ceil_to(stop, LANES)


def pair_plan(head_count, own_rows, fresh_rows, chunks):
    ratio = 2 * own_rows // fresh_rows
    shipped = head_count // (1 + ratio)
    asked = head_count - shipped
    if shipped % (2 * chunks) or asked % (2 * chunks):
        return None
    if asked * fresh_rows != shipped * 2 * own_rows:
        return None
    if own_rows % LANES or fresh_rows % LANES:
        return None
    a, s = asked // chunks, shipped // chunks
    return [
        (
            tuple(range(c * a, (c + 1) * a)),
            tuple(range(asked + c * s, asked + (c + 1) * s)),
        )
        for c in range(chunks)
    ]


def pair_body(
    plan,
    tokens,
    projection_weight,
    shift_term,
    scale_term,
    query_gain,
    key_gain,
    stale_keys,
    stale_values,
    stale_output,
    refreshed,
):
    (
        tokens,
        projection_weight,
        shift_term,
        scale_term,
        query_gain,
        key_gain,
        stale_keys,
        stale_values,
        stale_output,
        refreshed,
    ) = (
        pltpu.with_memory_space_constraint(array, pltpu.HBM)
        for array in (
            tokens,
            projection_weight,
            shift_term,
            scale_term,
            query_gain,
            key_gain,
            stale_keys,
            stale_values,
            stale_output,
            refreshed,
        )
    )
    N, D = tokens.shape
    HD = query_gain.shape[0]
    heads = D // HD
    tiles = N // TILE
    patch_count = lax.axis_size("patch")
    R = tiles * patch_count // 3 * TILE
    HP = ceil_to(HD + 1, 16)
    f32, bf16 = jnp.float32, jnp.bfloat16
    factor = math.log2(math.e) / math.sqrt(HD)
    asked = [h for qs, _ in plan for h in qs]
    shipped = [h for _, ks in plan for h in ks]
    hq, hk = len(plan[0][0]), len(plan[0][1])
    qrows, krows = hq * HD, 2 * hk * HD
    xrows = qrows * (R // LANES)
    trows = ceil_to(hq, 8)
    rrows = xrows + ceil_to(2 * trows * (R // LANES), 16)
    VM = pl.BlockSpec(memory_space=pltpu.VMEM)
    ANY = pl.BlockSpec(memory_space=pl.ANY)
    SM = pl.BlockSpec(memory_space=pltpu.SMEM)
    params = pltpu.CompilerParams(vmem_limit_bytes=28 * 1024 * 1024)
    DMA = pltpu.SemaphoreType.DMA
    vm = pltpu.VMEM

    def sds(rows, cols, dtype):
        return jax.ShapeDtypeStruct((rows, cols), dtype)

    def near(rows, cols, dtype):
        return pltpu.VMEM((rows, cols), dtype)

    def here(array):
        return pltpu.with_memory_space_constraint(array, pltpu.VMEM)

    def is_fresh(flags):
        base = lax.axis_index("patch") * tiles
        return lax.fori_loop(0, tiles, lambda t, s: s + flags[base + t], 0) > 0

    def each_tile(flags, action):
        base = lax.axis_index("patch") * tiles

        def step(t, seen):
            flag = flags[base + t]

            @pl.when(flag > 0)
            def _():
                action(pl.multiple_of(t * TILE, TILE), pl.multiple_of(seen * TILE, TILE))

            return seen + flag

        lax.fori_loop(0, tiles, step, 0)

    def column(gain):
        row = jnp.broadcast_to(gain[...].reshape(1, HD), (HD, HD))
        eye = lax.broadcasted_iota(jnp.int32, (HD, HD), 0) == lax.broadcasted_iota(
            jnp.int32, (HD, HD), 1
        )
        return jnp.sum(jnp.where(eye, row, 0.0), axis=1, keepdims=True)

    def turn(source, width, target):
        for j in range(width // LANES):
            target[LANES * j : LANES * (j + 1), :] = source[:, LANES * j : LANES * (j + 1)].astype(f32).T

    def normed(part, gain):
        spread = jnp.mean(part * part, axis=0, keepdims=True)
        return part * lax.rsqrt(spread + epsilon) * gain

    def padded(part, fill):
        extra = jnp.full((HP - HD, part.shape[1]), fill, f32)
        return jnp.concatenate([part, extra], axis=0).astype(bf16)

    def put(target, row, stride, value):
        for b in range(value.shape[1] // LANES):
            target[stride * b + row : stride * b + row + value.shape[0], :] = value[
                :, LANES * b : LANES * (b + 1)
            ]

    def take(source, row, stride, count, width):
        return jnp.concatenate(
            [source[stride * b + row : stride * b + row + count, :] for b in range(width // LANES)],
            axis=1,
        ).astype(f32)

    def pack_queries(projected_turned, low, qs, gain, target):
        for i in range(0, len(qs), 2):
            two = [
                normed(projected_turned[HD * h - low : HD * (h + 1) - low, :], gain)
                for h in qs[i : i + 2]
            ]
            put(target, HD * i, qrows, jnp.concatenate(two, axis=0).astype(bf16))

    def pack_shipped(kbuf, vbuf, turned, low, ks, gain, target):
        width = kbuf.shape[1]
        turn(kbuf, width, turned)
        for i in range(0, len(ks), 2):
            two = [normed(turned[HD * h - low : HD * (h + 1) - low, :], gain) for h in ks[i : i + 2]]
            put(target, HD * i, krows, jnp.concatenate(two, axis=0).astype(bf16))
        turn(vbuf, width, turned)
        for i in range(0, len(ks), 2):
            two = [turned[HD * h - low : HD * (h + 1) - low, :] for h in ks[i : i + 2]]
            put(target, HD * (len(ks) + i), krows, jnp.concatenate(two, axis=0).astype(bf16))

    def score(queries, keys, values):
        scores = lax.dot_general(
            keys, queries, (((0,), (0,)), ((), ())), preferred_element_type=f32
        )
        weights = jnp.exp2(scores * factor).astype(bf16)
        return jnp.dot(values, weights, preferred_element_type=f32)

    qlow0, qhigh0 = lane_window(HD * plan[0][0][0], HD * (plan[0][0][-1] + 1))
    qlow1, qhigh1 = lane_window(HD * (hq if len(plan) > 1 else shipped[0]), D)
    swindow = [lane_window(HD * ks[0], HD * (ks[-1] + 1)) for _, ks in plan]
    swidth = max(b - a for a, b in swindow)

    def front(flags, tok, w, shift, scale, gq, gk, sk, sv, x0, hid, xbuf, wbuf, qt, kbuf, vbuf, st, sems):
        fresh = is_fresh(flags)

        @pl.when(fresh)
        def _():
            wcopy = pltpu.make_async_copy(w.at[:, qlow0:qhigh0], wbuf, sems.at[0])
            each_tile(
                flags,
                lambda t, s: pltpu.make_async_copy(
                    tok.at[pl.ds(t, TILE), :], xbuf.at[pl.ds(s, TILE), :], sems.at[1]
                ).start(),
            )
            wcopy.start()
            pltpu.make_async_copy(tok.at[0:R, :], xbuf, sems.at[1]).wait()
            up = 1.0 + scale[...].reshape(1, D)
            down = shift[...].reshape(1, D)
            for i in range(0, R, 64):
                x = xbuf[i : i + 64, :].astype(f32)
                center = x - jnp.mean(x, axis=1, keepdims=True)
                spread = jnp.mean(center * center, axis=1, keepdims=True)
                hid[i : i + 64, :] = (center * lax.rsqrt(spread + epsilon) * up + down).astype(bf16)
            wcopy.wait()
            projected = jnp.dot(hid[...], wbuf[...], preferred_element_type=f32).astype(bf16)
            turn(projected, qhigh0 - qlow0, qt)
            pack_queries(qt, qlow0, plan[0][0], column(gq), x0)

        @pl.when(jnp.logical_not(fresh))
        def _():
            low, high = swindow[0]
            kcopy = pltpu.make_async_copy(sk.at[:, low:high], kbuf, sems.at[0])
            vcopy = pltpu.make_async_copy(sv.at[:, low:high], vbuf, sems.at[1])
            kcopy.start()
            vcopy.start()
            kcopy.wait()
            vcopy.wait()
            pack_shipped(kbuf, vbuf, st, low, plan[0][1], column(gk), x0)

    width0 = swindow[0][1] - swindow[0][0]
    x0, hidden = pl.pallas_call(
        front,
        out_shape=(near(xrows, LANES, bf16), near(R, D, bf16)),
        in_specs=[SM, ANY, ANY, VM, VM, VM, VM, ANY, ANY],
        out_specs=(VM, VM),
        scratch_shapes=[
            vm((R, D), bf16),
            vm((D, qhigh0 - qlow0), bf16),
            vm((qhigh0 - qlow0, R), f32),
            vm((N, width0), bf16),
            vm((N, width0), bf16),
            vm((width0, N), f32),
            DMA((2,)),
        ],
        compiler_params=params,
        name="front",
    )(refreshed, tokens, projection_weight, shift_term, scale_term, query_gain, key_gain, stale_keys, stale_values)

    swap = [(0, 1), (1, 0)]

    def send(array):
        return lax.ppermute(array, "patch", swap)

    sent = [x0]
    got = [send(x0)]

    more = len(plan) > 1

    def second(flags, hid, w, gq, gk, sk, sv, *rest):
        x1 = rest[0] if more else None
        qx, wbuf, qt, kbuf, vbuf, st, sems = rest[1:] if more else rest
        fresh = is_fresh(flags)

        @pl.when(fresh)
        def _():
            wcopy = pltpu.make_async_copy(w.at[:, qlow1:qhigh1], wbuf, sems.at[0])
            wcopy.start()
            wcopy.wait()
            projected = jnp.dot(hid[...], wbuf[...], preferred_element_type=f32).astype(bf16)
            turn(projected, qhigh1 - qlow1, qt)
            gain = column(gq)
            if more:
                pack_queries(qt, qlow1, plan[1][0], gain, x1)
            for i, h in enumerate(shipped):
                part = normed(qt[HD * h - qlow1 : HD * (h + 1) - qlow1, :], gain)
                qx[HP * i : HP * (i + 1), :] = padded(part, 0.0)

        if more:

            @pl.when(jnp.logical_not(fresh))
            def _():
                low, high = swindow[1]
                kcopy = pltpu.make_async_copy(sk.at[:, low:high], kbuf, sems.at[0])
                vcopy = pltpu.make_async_copy(sv.at[:, low:high], vbuf, sems.at[1])
                kcopy.start()
                vcopy.start()
                kcopy.wait()
                vcopy.wait()
                pack_shipped(kbuf, vbuf, st, low, plan[1][1], column(gk), x1)

    width1 = swindow[-1][1] - swindow[-1][0]
    outs = [near(len(shipped) * HP, R, bf16)]
    if more:
        outs = [near(xrows, LANES, bf16)] + outs
    outs = pl.pallas_call(
        second,
        out_shape=tuple(outs),
        in_specs=[SM, VM, ANY, VM, VM, ANY, ANY],
        out_specs=(VM,) * len(outs),
        scratch_shapes=[
            vm((D, qhigh1 - qlow1), bf16),
            vm((qhigh1 - qlow1, R), f32),
            vm((N, width1), bf16),
            vm((N, width1), bf16),
            vm((width1, N), f32),
            DMA((2,)),
        ],
        compiler_params=params,
        name="second",
    )(refreshed, here(hidden), projection_weight, query_gain, key_gain, stale_keys, stale_values)
    if more:
        sent.append(outs[0])
        got.append(send(outs[0]))
    qx = outs[-1]

    def third(flags, hid, w, gk, sk, sv, so, kt, vt, out, kall, vall, new, wk, wv, turned, held, sems):
        fresh = is_fresh(flags)
        incopy = pltpu.make_async_copy(so, held, sems.at[0])
        ocopy = pltpu.make_async_copy(held, out, sems.at[0])
        kcopy = pltpu.make_async_copy(sk, kall, sems.at[1])
        vcopy = pltpu.make_async_copy(sv, vall, sems.at[2])
        kcopy.start()
        vcopy.start()

        @pl.when(fresh)
        def _():
            wkcopy = pltpu.make_async_copy(w.at[:, D : 2 * D], wk, sems.at[3])
            wvcopy = pltpu.make_async_copy(w.at[:, 2 * D : 3 * D], wv, sems.at[4])
            wkcopy.start()
            wvcopy.start()
            kcopy.wait()
            wkcopy.wait()
            new[...] = jnp.dot(hid[...], wk[...], preferred_element_type=f32).astype(bf16)

            def merge_keys(t, s):
                kall[pl.ds(t, TILE), :] = new[pl.ds(s, TILE), :]

            each_tile(flags, merge_keys)
            vcopy.wait()
            wvcopy.wait()
            new[...] = jnp.dot(hid[...], wv[...], preferred_element_type=f32).astype(bf16)

            def merge_values(t, s):
                vall[pl.ds(t, TILE), :] = new[pl.ds(s, TILE), :]

            each_tile(flags, merge_values)

        @pl.when(jnp.logical_not(fresh))
        def _():
            kcopy.wait()
            vcopy.wait()

        incopy.start()
        gain = column(gk)
        turn(kall, D, turned)
        for h in range(heads):
            kt[HP * h : HP * (h + 1), :] = padded(normed(turned[HD * h : HD * (h + 1), :], gain), 0.0)
        incopy.wait()
        ocopy.start()
        turn(vall, D, turned)
        for h in range(heads):
            vt[HP * h : HP * (h + 1), :] = padded(turned[HD * h : HD * (h + 1), :], 1.0)
        ocopy.wait()

    kt, vt, held = pl.pallas_call(
        third,
        out_shape=(near(heads * HP, N, bf16), near(heads * HP, N, bf16), sds(N, D, bf16)),
        in_specs=[SM, VM, ANY, VM, ANY, ANY, ANY],
        out_specs=(VM, VM, ANY),
        scratch_shapes=[
            vm((N, D), bf16),
            vm((N, D), bf16),
            vm((R, D), bf16),
            vm((D, D), bf16),
            vm((D, D), bf16),
            vm((D, N), f32),
            vm((N, D), bf16),
            DMA((5,)),
        ],
        compiler_params=params,
        name="third",
    )(refreshed, here(hidden), projection_weight, key_gain, stale_keys, stale_values, stale_output)

    def query_pair(x, i):
        two = take(x, HD * i, qrows, 2 * HD, R)
        return [padded(two[:HD], 0.0), padded(two[HD:], 0.0)]

    def keys_of(kt, h):
        return kt[HP * h : HP * (h + 1), :]

    def answer(x, kt, vt, qs, target):
        totals = []
        for i in range(0, hq, 2):
            both = []
            for q, h in zip(query_pair(x, i), qs[i : i + 2]):
                terms = score(q, keys_of(kt, h), keys_of(vt, h))
                both.append(terms[:HD])
                totals.append(terms[HD : HD + 1])
            put(target, HD * i, qrows, jnp.concatenate(both, axis=0).astype(bf16))
        if trows > hq:
            totals.append(jnp.zeros((trows - hq, R), f32))
        total = jnp.concatenate(totals, axis=0)
        high = total.astype(bf16)
        low = (total - high.astype(f32)).astype(bf16)
        pieces = [
            piece[:, LANES * b : LANES * (b + 1)].astype(f32)
            for piece in (high, low)
            for b in range(R // LANES)
        ]
        spare = rrows - xrows - len(pieces) * trows
        if spare:
            pieces.append(jnp.zeros((spare, LANES), f32))
        target[xrows:, :] = jnp.concatenate(pieces, axis=0).astype(bf16)

    def own_terms_of(x, kt, vt, qs, target):
        for i in range(0, hq, 2):
            for k, (q, h) in enumerate(zip(query_pair(x, i), qs[i : i + 2])):
                target[HP * (i + k) : HP * (i + k + 1), :] = score(q, keys_of(kt, h), keys_of(vt, h))

    answers, own = [], []
    for c, (qs, _) in enumerate(plan):

        def reply(flags, xr, kt, vt, *rest, c=c, qs=qs):
            fresh = is_fresh(flags)
            if c:
                xs, r, mine = rest
            else:
                (r,) = rest

            @pl.when(jnp.logical_not(fresh))
            def _():
                answer(xr, kt, vt, qs, r)

            if c:

                @pl.when(fresh)
                def _():
                    own_terms_of(xs, kt, vt, plan[c - 1][0], mine)

        extra = [sent[c - 1]] if c else []
        res = pl.pallas_call(
            reply,
            out_shape=(near(rrows, LANES, bf16),) + ((near(hq * HP, R, f32),) if c else ()),
            in_specs=[SM, VM, VM, VM] + [VM] * len(extra),
            out_specs=(VM,) * (1 + len(extra)),
            compiler_params=params,
        )(refreshed, here(got[c]), here(kt), here(vt), *map(here, extra))
        answers.append(send(res[0]))
        if c:
            own.append(res[1])

    def rest_of(flags, xs, kt, vt, qx, *rest):
        xr = rest[: len(plan)]
        mine, full = rest[len(plan) :]

        @pl.when(is_fresh(flags))
        def _():
            own_terms_of(xs, kt, vt, plan[-1][0], mine)
            for c, (_, ks) in enumerate(plan):
                for i in range(0, hk, 2):
                    ktwo = take(xr[c], HD * i, krows, 2 * HD, N)
                    vtwo = take(xr[c], HD * (hk + i), krows, 2 * HD, N)
                    for k in range(2):
                        h = ks[i + k]
                        at = shipped.index(h)
                        q = qx[HP * at : HP * (at + 1), :]
                        terms = score(q, keys_of(kt, h), keys_of(vt, h)) + score(
                            q,
                            padded(ktwo[HD * k : HD * (k + 1)], 0.0),
                            padded(vtwo[HD * k : HD * (k + 1)], 1.0),
                        )
                        full[HD * at : HD * (at + 1), :] = terms[:HD] / terms[HD : HD + 1]

    mine, full = pl.pallas_call(
        rest_of,
        out_shape=(near(hq * HP, R, f32), near(len(shipped) * HD, R, f32)),
        in_specs=[SM, VM, VM, VM, VM] + [VM] * len(plan),
        out_specs=(VM, VM),
        compiler_params=params,
        name="rest",
    )(refreshed, here(sent[-1]), here(kt), here(vt), here(qx), *map(here, got))
    own.append(mine)

    def last(flags, full, *rest):
        mine = rest[: len(plan)]
        theirs = rest[len(plan) : 2 * len(plan)]
        _, out, turned, rows, sem = rest[2 * len(plan) :]

        @pl.when(is_fresh(flags))
        def _():
            turned[HD * shipped[0] :, :] = full[...]
            blocks = R // LANES
            for c, (qs, _) in enumerate(plan):
                tail = theirs[c][xrows:, :].astype(f32)
                parts = [tail[trows * k : trows * (k + 1)] for k in range(2 * blocks)]
                total = jnp.concatenate(
                    [parts[b] + parts[blocks + b] for b in range(blocks)], axis=1
                )
                for i in range(0, hq, 2):
                    two = take(theirs[c], HD * i, qrows, 2 * HD, R)
                    for k in range(2):
                        h = i + k
                        terms = mine[c][HP * h : HP * (h + 1), :]
                        top = terms[:HD] + two[HD * k : HD * (k + 1)]
                        bottom = terms[HD : HD + 1] + total[h : h + 1]
                        turned[HD * qs[h] : HD * (qs[h] + 1), :] = top / bottom
            for j in range(D // LANES):
                rows[:, LANES * j : LANES * (j + 1)] = turned[LANES * j : LANES * (j + 1), :].T.astype(bf16)
            each_tile(
                flags,
                lambda t, s: pltpu.make_async_copy(
                    rows.at[pl.ds(s, TILE), :], out.at[pl.ds(t, TILE), :], sem
                ).start(),
            )
            pltpu.make_async_copy(rows, out.at[0:R, :], sem).wait()

    operands = (refreshed, *map(here, (full, *own, *answers)), held)
    return pl.pallas_call(
        last,
        out_shape=sds(N, D, bf16),
        in_specs=[SM] + [VM] * (1 + 2 * len(plan)) + [ANY],
        out_specs=ANY,
        input_output_aliases={len(operands) - 1: 0},
        scratch_shapes=[vm((D, R), f32), vm((R, D), bf16), DMA],
        compiler_params=params,
        name="last",
    )(*operands)


def pick_plan(mesh, tokens_shape):
    patch = mesh.shape["patch"]
    own_rows = tokens_shape // (mesh.shape["grp"] * patch)
    own_tiles = own_rows // TILE
    fresh_tiles = own_tiles * patch // 3
    if patch != 2 or fresh_tiles > own_tiles:
        return None
    return pair_plan(H, own_rows, fresh_tiles * TILE, CHUNKS)


CHUNKS = 2


def solution(mesh):
    in_specs = (
        P(("grp", "patch"), None),
        P(),
        P(),
        P(),
        P(),
        P(),
        P(("grp", "patch"), None),
        P(("grp", "patch"), None),
        P(("grp", "patch"), None),
        P("grp"),
    )
    out_specs = P(("grp", "patch"), None)

    def whole(*arrays):
        plan = pick_plan(mesh, arrays[0].shape[0])
        if plan is None:
            inner = body
        else:

            def inner(*blocks):
                return pair_body(plan, *blocks)

        step = jax.shard_map(
            inner, mesh=mesh, in_specs=in_specs, out_specs=out_specs, check_vma=False
        )
        return step(*arrays)

    return whole
```

```python
import math

import jax
import jax.numpy as jnp
from jax import lax
from jax.experimental import pallas as pl
from jax.experimental.pallas import tpu as pltpu
from jax.sharding import PartitionSpec as P


H = 16
TILE = 16


epsilon = 1e-06


def modulate(row_block, shift_term, scale_term):
    values = row_block.astype(jnp.float32)
    center = values - jnp.mean(values, axis=-1, keepdims=True)
    spread = jnp.mean(center * center, axis=-1, keepdims=True)
    normed = center / jnp.sqrt(spread + epsilon)
    return (normed * (1.0 + scale_term) + shift_term).astype(jnp.bfloat16)


def head_norm(row_block, gain_vector, head_count):
    values = row_block.astype(jnp.float32).reshape(row_block.shape[0], head_count, -1)
    normed = values / jnp.sqrt(jnp.mean(values * values, axis=-1, keepdims=True) + epsilon)
    return (normed * gain_vector).astype(jnp.bfloat16).reshape(row_block.shape[0], -1)


def block_size(row_total, row_unit):
    multiple = row_total // row_unit
    chosen = 1
    for candidate in range(1, multiple + 1):
        if multiple % candidate == 0 and candidate * row_unit <= 1024:
            chosen = candidate
    return chosen * row_unit


def partial_terms(queries, key_rows, values, head_count):
    query_count = queries.shape[0]
    model_width = queries.shape[1]
    head_size = model_width // head_count
    factor = 1.0 / math.sqrt(head_size)
    query_heads = queries.reshape(query_count, head_count, head_size)
    key_heads = key_rows.reshape(key_rows.shape[0], head_count, head_size)
    value_heads = values.reshape(values.shape[0], head_count, head_size)
    scores = (
        jnp.einsum("qhd,khd->hqk", query_heads, key_heads, preferred_element_type=jnp.float32)
        * factor
    )
    weights = jnp.exp(scores)
    totals = jnp.sum(weights, axis=2).T
    numerator = jnp.einsum(
        "hqk,khd->qhd",
        weights.astype(jnp.bfloat16),
        value_heads,
        preferred_element_type=jnp.float32,
    )
    return (numerator.reshape(query_count, model_width), totals)


def own_terms(every_query, key_rows, values, head_count, row_unit):
    row_total = every_query.shape[0]
    stride = block_size(row_total, row_unit)

    def advance(turn_index, inner_sums):
        offset = turn_index * stride
        query_block = lax.dynamic_slice_in_dim(every_query, offset, stride, 0)
        numerator, totals = partial_terms(query_block, key_rows, values, head_count)
        return (
            lax.dynamic_update_slice_in_dim(inner_sums[0], numerator, offset, 0),
            lax.dynamic_update_slice_in_dim(inner_sums[1], totals, offset, 0),
        )

    starting = (
        jnp.zeros((row_total, key_rows.shape[1]), jnp.float32),
        jnp.zeros((row_total, head_count), jnp.float32),
    )
    return lax.fori_loop(0, row_total // stride, advance, starting)


def attend(queries, own_keys, own_values, head_count):
    query_count = queries.shape[0]
    model_width = queries.shape[1]
    every_query = lax.all_gather(queries, "patch", axis=0, tiled=True)
    numerator, totals = own_terms(every_query, own_keys, own_values, head_count, query_count)
    numerator, totals = (
        lax.psum_scatter(
            numerator.astype(jnp.bfloat16), "patch", scatter_dimension=0, tiled=True
        ).astype(jnp.float32),
        lax.psum_scatter(
            totals.astype(jnp.bfloat16), "patch", scatter_dimension=0, tiled=True
        ).astype(jnp.float32),
    )
    fresh_heads = numerator.reshape(query_count, head_count, -1) / totals[:, :, None]
    return fresh_heads.reshape(query_count, model_width).astype(jnp.bfloat16)


def body(
    tokens,
    projection_weight,
    shift_term,
    scale_term,
    query_gain,
    key_gain,
    stale_keys,
    stale_values,
    stale_output,
    refreshed,
):
    model_width = tokens.shape[1]
    head_count = H
    own_rows = tokens.shape[0]
    own_tiles = own_rows // TILE
    patch_count = lax.axis_size("patch")
    my_index = lax.axis_index("patch")
    share_tiles = own_tiles // 3
    most_tiles = min(own_tiles, share_tiles * patch_count)
    tile_grid = refreshed.reshape(patch_count, own_tiles)
    my_tiles = lax.dynamic_index_in_dim(tile_grid, my_index, 0, keepdims=False)
    picked = jnp.nonzero(my_tiles, size=most_tiles, fill_value=0)[0].astype(jnp.int32)
    token_tiles = tokens.reshape(own_tiles, TILE, model_width)
    chosen = token_tiles[picked].reshape(most_tiles * TILE, model_width)
    hidden = modulate(chosen, shift_term, scale_term)
    projected = jnp.dot(hidden, projection_weight, preferred_element_type=jnp.float32)
    query_new = projected[:, :model_width].astype(jnp.bfloat16)
    key_new = (
        projected[:, model_width : 2 * model_width]
        .astype(jnp.bfloat16)
        .reshape(most_tiles, TILE, model_width)
    )
    value_new = (
        projected[:, 2 * model_width :].astype(jnp.bfloat16).reshape(most_tiles, TILE, model_width)
    )
    position = jnp.maximum(jnp.cumsum(my_tiles) - 1, 0)
    fresh_tile = (my_tiles > 0)[:, None, None]
    keys_all = jnp.where(
        fresh_tile, key_new[position], stale_keys.reshape(own_tiles, TILE, model_width)
    ).reshape(own_rows, model_width)
    values_all = jnp.where(
        fresh_tile, value_new[position], stale_values.reshape(own_tiles, TILE, model_width)
    ).reshape(own_rows, model_width)
    own_keys = head_norm(keys_all, key_gain, head_count)
    queries = head_norm(query_new, query_gain, head_count)
    fresh_rows = attend(queries, own_keys, values_all, head_count)
    fresh_tiles = fresh_rows.reshape(most_tiles, TILE, model_width)
    merged = jnp.where(
        fresh_tile, fresh_tiles[position], stale_output.reshape(own_tiles, TILE, model_width)
    )
    return merged.reshape(own_rows, model_width)


LANES = 128
SENDS = 2


def ceil_to(amount, unit):
    return -(-amount // unit) * unit


def pair_plan(head_count, model_width, own_rows, fresh_rows):
    head_size = model_width // head_count
    ratio = 2 * own_rows // fresh_rows
    if 2 * own_rows % fresh_rows or own_rows % LANES or fresh_rows % LANES:
        return None
    if head_count % (SENDS * (1 + ratio)):
        return None
    if head_size % 8 or fresh_rows // LANES * head_size % 16 or 2 * own_rows // LANES * head_size % 16:
        return None
    parts = head_count // (SENDS * (1 + ratio))
    asked = SENDS * parts * ratio
    chunks = [tuple(range(h, h + parts * ratio)) for h in range(0, asked, parts * ratio)]
    shipped = [tuple(range(h, h + parts)) for h in range(asked, head_count, parts)]
    cut = -(-2 * len(chunks[-1]) // 3)
    answers = [(c, qs) for c, qs in enumerate(chunks[:-1])]
    answers += [(SENDS - 1, chunks[-1][:cut]), (SENDS - 1, chunks[-1][cut:])]
    return chunks, shipped, answers


def pair_body(
    plan,
    tokens,
    projection_weight,
    shift_term,
    scale_term,
    query_gain,
    key_gain,
    stale_keys,
    stale_values,
    stale_output,
    refreshed,
):
    chunks, parcels, answers = plan
    shipped = [h for ks in parcels for h in ks]
    N, D = tokens.shape
    HD = query_gain.shape[0]
    heads = D // HD
    tiles = N // TILE
    R = tiles * lax.axis_size("patch") // 3 * TILE
    fresh_tiles = R // TILE
    HP = ceil_to(HD + 1, 16)
    QB, KB = R // LANES, N // LANES
    QR = QB * HD
    f32, bf16 = jnp.float32, jnp.bfloat16
    factor = math.log2(math.e) / math.sqrt(HD)
    asked = shipped[0]
    DMA = pltpu.SemaphoreType.DMA
    vm = pltpu.VMEM
    VM = pl.BlockSpec(memory_space=pltpu.VMEM)
    SM = pl.BlockSpec(memory_space=pltpu.SMEM)
    ANY = pl.BlockSpec(memory_space=pl.ANY)
    params = pltpu.CompilerParams(vmem_limit_bytes=28 * 1024 * 1024)

    def far(array):
        return pltpu.with_memory_space_constraint(array, pltpu.HBM)

    def here(array):
        return pltpu.with_memory_space_constraint(array, pltpu.VMEM)

    def near(rows, cols, dtype):
        return pltpu.VMEM((rows, cols), dtype)

    def call(kernel, outs, out_specs, ins, in_specs, scratch=(), aliases=None):
        return pl.pallas_call(
            kernel,
            out_shape=tuple(outs),
            in_specs=list(in_specs),
            out_specs=tuple(out_specs),
            scratch_shapes=list(scratch),
            input_output_aliases=aliases or {},
            compiler_params=params,
        )(*ins)

    def tail_rows(n):
        return ceil_to(2 * QB * n, 16)

    def wide(column, width):
        return jnp.concatenate([column] * (width // LANES), axis=1)

    def normed(part, gain):
        spread = jnp.mean(part * part, axis=0, keepdims=True)
        return part * lax.rsqrt(spread + epsilon) * wide(gain, part.shape[1])

    def padded(part, fill):
        extra = jnp.full((HP - HD, part.shape[1]), fill, f32)
        return jnp.concatenate([part, extra], axis=0).astype(bf16)

    def turn(source, low, high, target):
        for j in range(low, high, LANES):
            target[j - low : j - low + LANES, :] = source[:, j : j + LANES].astype(f32).T

    def pieces(parts):
        return jnp.concatenate(
            [p[:, b : b + LANES] for p in parts for b in range(0, p.shape[1], LANES)], axis=0
        ).astype(bf16)

    def widen(block, first, count):
        return jnp.concatenate(
            [block[HD * (first + b) : HD * (first + b + 1), :] for b in range(count)], axis=1
        )

    def query_of(x, i):
        return padded(widen(x[QR * i : QR * (i + 1), :].astype(f32), 0, QB), 0.0)

    def score(queries, keys, values):
        scores = lax.dot_general(
            queries, keys, (((0,), (0,)), ((), ())), preferred_element_type=f32
        )
        weights = jnp.exp2(scores * factor).astype(bf16)
        return lax.dot_general(
            values, weights, (((1,), (1,)), ((), ())), preferred_element_type=f32
        )

    def head_of(ref, h):
        return ref[HP * h : HP * (h + 1), :]

    high0 = ceil_to(HD * (chunks[0][-1] + 1), LANES)
    low1 = HD * chunks[1][0] // LANES * LANES
    lows = HD * shipped[0] // LANES * LANES

    def answer(x, skip, kt, vt, qs, target):
        n = len(qs)
        count = tail_rows(n)
        place = lax.broadcasted_iota(jnp.int32, (count, LANES), 0)
        tail = jnp.zeros((count, LANES), f32)
        for i, h in enumerate(qs):
            terms = score(query_of(x, skip + i), head_of(kt, h), head_of(vt, h))
            target[QR * i : QR * (i + 1), :] = pieces([terms[:HD]])
            total = terms[HD : HD + 1]
            top = total.astype(bf16).astype(f32)
            for k, piece in enumerate((top, total - top)):
                for b in range(QB):
                    row = (2 * i + k) * QB + b
                    tail = jnp.where(place == row, piece[:, LANES * b : LANES * (b + 1)], tail)
        target[QR * n : QR * n + count, :] = tail.astype(bf16)

    def total_of(tail, i):
        parts = [
            tail[(2 * i) * QB + b : (2 * i) * QB + b + 1, :]
            + tail[(2 * i + 1) * QB + b : (2 * i + 1) * QB + b + 1, :]
            for b in range(QB)
        ]
        return jnp.concatenate(parts, axis=1)

    groups = [tuple(range(heads // 2)), tuple(range(heads // 2, heads))]

    def own_terms(own, h):
        g = 0 if h in groups[0] else 1
        i = h - groups[g][0]
        return own[g][HP * i : HP * (i + 1), :]

    def own_query(h, sent, qx):
        if h >= asked:
            return qx[HP * (h - asked) : HP * (h - asked + 1), :]
        c = [h in qs for qs in chunks].index(True)
        return query_of(sent[c], h - chunks[c][0])

    def settle(info, new, mix):
        for i in range(fresh_tiles):
            mix[pl.ds(pl.multiple_of(info[1 + i], TILE), TILE), :] = new[TILE * i : TILE * (i + 1), :]

    def merge(own_terms, x, qs, target, low):
        tail = x[QR * len(qs) : QR * len(qs) + tail_rows(len(qs)), :].astype(f32)
        for i, h in enumerate(qs):
            terms = own_terms(h)
            theirs = widen(x[QR * i : QR * (i + 1), :].astype(f32), 0, QB)
            target[HD * h - low : HD * (h + 1) - low, :] = (terms[:HD] + theirs) / (
                terms[HD : HD + 1] + total_of(tail, i)
            )

    def write_rows(info, rows, out, low, high, sem):
        if low == high:
            return
        for i in range(fresh_tiles):
            pltpu.make_async_copy(
                rows.at[TILE * i : TILE * (i + 1), low:high],
                out.at[pl.ds(pl.multiple_of(info[1 + i], TILE), TILE), low:high],
                sem,
            ).start()

    def wait_rows(rows, out, low, high, sem):
        if low == high:
            return
        pltpu.make_async_copy(rows.at[:, low:high], out.at[0:R, low:high], sem).wait()

    def turn_back(turned, low, rows, j):
        rows[:, j : j + LANES] = turned[j - low : j - low + LANES, :].T.astype(bf16)

    block_rows = 2 * KB * HD

    def front(
        flags, tok, w, shift, scale, gq, gk, sk, sv,
        info, gains, hid, wq, x0, kv,
        fl, sh, sc, g0, g1, tbuf, wbuf, kbuf, vbuf, qt, st, sems,
    ):
        def load(source, target, k):
            copy = pltpu.make_async_copy(source, target, sems.at[k])
            copy.start()
            return copy

        cflags = load(flags, fl, 0)
        cg0 = load(gq, g0, 1)
        cg1 = load(gk, g1, 2)
        ck = load(sk.at[:, lows:D], kbuf, 3)
        cv = load(sv.at[:, lows:D], vbuf, 4)
        ctok = load(tok, tbuf, 5)
        cshift = load(shift, sh, 6)
        cscale = load(scale, sc, 7)
        cw = load(w.at[:, 0:high0], wbuf, 8)
        cflags.wait()
        me = lax.axis_index("patch")
        base = me * tiles

        def note(t, seen):
            info[1 + seen] = t * TILE
            return seen + fl[base + t]

        count = lax.fori_loop(0, tiles, note, 0)
        info[0] = count
        rest = pltpu.make_async_copy(w.at[:, low1:D], wq, sems.at[9])

        @pl.when(count > 0)
        def _():
            rest.start()

        cg0.wait()
        cg1.wait()
        eye = lax.broadcasted_iota(jnp.int32, (HD, HD), 0) == lax.broadcasted_iota(
            jnp.int32, (HD, HD), 1
        )
        for k, g in enumerate((g0, g1)):
            row = jnp.broadcast_to(g[...].reshape(1, HD), (HD, HD))
            column = jnp.sum(jnp.where(eye, row, 0.0), axis=1, keepdims=True)
            gains[HD * k : HD * (k + 1), :] = jnp.broadcast_to(column, (HD, LANES))
        ck.wait()
        cv.wait()

        @pl.when(count == 0)
        def _():
            turn(kbuf, 0, D - lows, st.at[0])
            turn(vbuf, 0, D - lows, st.at[1])
            gain = gains[HD : 2 * HD, :]
            for c, ks in enumerate(parcels):
                for i, h in enumerate(ks):
                    at = HD * h - lows
                    block = pieces([normed(st[0, at : at + HD, :], gain), st[1, at : at + HD, :]])
                    if c == 0:
                        x0[block_rows * i : block_rows * (i + 1), :] = block
                    else:
                        row = block_rows * ((c - 1) * len(ks) + i)
                        kv[row : row + block_rows, :] = block

        cshift.wait()
        cscale.wait()
        ctok.wait()

        @pl.when(count > 0)
        def _():
            up = 1.0 + sc[...].reshape(1, D)
            down = sh[...].reshape(1, D)
            for i in range(fresh_tiles):
                x = tbuf[pl.ds(pl.multiple_of(info[1 + i], TILE), TILE), :].astype(f32)
                center = x - jnp.mean(x, axis=1, keepdims=True)
                spread = jnp.mean(center * center, axis=1, keepdims=True)
                hid[TILE * i : TILE * (i + 1), :] = (
                    center * lax.rsqrt(spread + epsilon) * up + down
                ).astype(bf16)

        cw.wait()

        @pl.when(count > 0)
        def _():
            projected = jnp.dot(hid[...], wbuf[...], preferred_element_type=f32).astype(bf16)
            turn(projected, 0, high0, qt)
            gain = gains[0:HD, :]
            for i, h in enumerate(chunks[0]):
                x0[QR * i : QR * (i + 1), :] = pieces([normed(qt[HD * h : HD * (h + 1), :], gain)])
            rest.wait()

    info, gains, hidden, wq, x0, kv = call(
        front,
        [
            pltpu.SMEM((fresh_tiles + 2,), jnp.int32),
            near(2 * HD, LANES, f32),
            near(R, D, bf16),
            near(D, D - low1, bf16),
            near(QR * len(chunks[0]), LANES, bf16),
            near(block_rows * (len(shipped) - len(parcels[0])), LANES, bf16),
        ],
        [SM] + [VM] * 5,
        [
            far(a)
            for a in (
                refreshed, tokens, projection_weight, shift_term, scale_term,
                query_gain, key_gain, stale_keys, stale_values,
            )
        ],
        [ANY] * 9,
        [
            pltpu.SMEM(refreshed.shape, jnp.int32),
            vm(shift_term.shape, f32),
            vm(scale_term.shape, f32),
            vm(query_gain.shape, f32),
            vm(key_gain.shape, f32),
            vm((N, D), bf16),
            vm((D, high0), bf16),
            vm((N, D - lows), bf16),
            vm((N, D - lows), bf16),
            vm((high0, R), f32),
            vm((2, D - lows, N), f32),
            DMA((10,)),
        ],
    )

    info = pltpu.with_memory_space_constraint(info, pltpu.SMEM)
    gains, hidden, wq = here(gains), here(hidden), here(wq)
    got = []

    def send(array):
        got.append(lax.ppermute(array, "patch", [(0, 1), (1, 0)]))

    send(x0)

    def second(
        info, gains, hid, wq, w, sk, sv, kv,
        x1, qx, kt, vt, wk, qt, kbuf, vbuf, turned, sems,
    ):
        @pl.when(info[0] > 0)
        def _():
            wcopy = pltpu.make_async_copy(w.at[:, D : 2 * D], wk, sems.at[0])
            wcopy.start()
            projected = jnp.dot(hid[...], wq[...], preferred_element_type=f32).astype(bf16)
            turn(projected, 0, D - low1, qt)
            gain = gains[0:HD, :]
            first = chunks[1][0]
            for h in range(first, heads):
                part = normed(qt[HD * h - low1 : HD * (h + 1) - low1, :], gain)
                if h < asked:
                    i = h - first
                    x1[QR * i : QR * (i + 1), :] = pieces([part])
                else:
                    i = h - asked
                    qx[HP * i : HP * (i + 1), :] = padded(part, 0.0)
            wcopy.wait()

        @pl.when(info[0] == 0)
        def _():
            width = ceil_to(HD * asked, LANES)
            kcopy = pltpu.make_async_copy(sk.at[:, 0:width], kbuf.at[:, 0:width], sems.at[0])
            vcopy = pltpu.make_async_copy(sv.at[:, 0:width], vbuf.at[:, 0:width], sems.at[1])
            kcopy.start()
            vcopy.start()
            x1[...] = kv[...]
            gain = gains[HD : 2 * HD, :]
            kcopy.wait()
            turn(kbuf, 0, width, turned)
            for h in range(asked):
                kt[HP * h : HP * (h + 1), :] = padded(normed(turned[HD * h : HD * (h + 1), :], gain), 0.0)
            vcopy.wait()
            turn(vbuf, 0, width, turned)
            for h in range(asked):
                vt[HP * h : HP * (h + 1), :] = padded(turned[HD * h : HD * (h + 1), :], 1.0)

    x1, qx, kt_far, vt_far, wk = call(
        second,
        [
            near(QR * len(chunks[1]), LANES, bf16),
            near(HP * len(shipped), R, bf16),
            near(HP * asked, N, bf16),
            near(HP * asked, N, bf16),
            near(D, D, bf16),
        ],
        [VM] * 5,
        [info, gains, hidden, wq, *map(far, (projection_weight, stale_keys, stale_values)), here(kv)],
        [SM, VM, VM, VM, ANY, ANY, ANY, VM],
        [vm((D - low1, R), f32), vm((N, D), bf16), vm((N, D), bf16), vm((D, N), f32), DMA((2,))],
    )
    qx, kt_far, vt_far, wk = map(here, (qx, kt_far, vt_far, wk))
    send(x1)
    sent = [here(x0), here(x1)]

    def third(
        info, gains, hid, wk, w, sk, sv, so,
        kt, vt, out, new, mix, wv, vmix, held, turned, sems,
    ):
        @pl.when(info[0] > 0)
        def _():
            kcopy = pltpu.make_async_copy(sk, mix, sems.at[0])
            kcopy.start()
            wcopy = pltpu.make_async_copy(w.at[:, 2 * D : 3 * D], wv, sems.at[1])
            wcopy.start()
            vcopy = pltpu.make_async_copy(sv, vmix, sems.at[2])
            vcopy.start()
            icopy = pltpu.make_async_copy(so, held, sems.at[3])
            icopy.start()
            ocopy = pltpu.make_async_copy(held, out, sems.at[4])
            new[...] = jnp.dot(hid[...], wk[...], preferred_element_type=f32).astype(bf16)
            kcopy.wait()
            settle(info, new, mix)
            turn(mix, 0, D, turned)
            gain = gains[HD : 2 * HD, :]
            for h in range(heads):
                kt[HP * h : HP * (h + 1), :] = padded(normed(turned[HD * h : HD * (h + 1), :], gain), 0.0)
            icopy.wait()
            ocopy.start()
            wcopy.wait()
            new[...] = jnp.dot(hid[...], wv[...], preferred_element_type=f32).astype(bf16)
            vcopy.wait()
            settle(info, new, vmix)
            turn(vmix, 0, D, turned)
            for h in range(heads):
                vt[HP * h : HP * (h + 1), :] = padded(turned[HD * h : HD * (h + 1), :], 1.0)
            ocopy.wait()

    kt, vt, out = call(
        third,
        [near(HP * heads, N, bf16), near(HP * heads, N, bf16), jax.ShapeDtypeStruct((N, D), bf16)],
        [VM, VM, ANY],
        [
            info, gains, hidden, wk,
            *map(far, (projection_weight, stale_keys, stale_values, stale_output)),
        ],
        [SM, VM, VM, VM, ANY, ANY, ANY, ANY],
        [
            vm((R, D), bf16),
            vm((N, D), bf16),
            vm((D, D), bf16),
            vm((N, D), bf16),
            vm((N, D), bf16),
            vm((D, N), f32),
            DMA((5,)),
        ],
    )
    kt, vt = here(kt), here(vt)

    own, told = [], []

    for a, (c, qs) in enumerate(answers):
        group = groups[a - SENDS + 1] if SENDS - 1 <= a < SENDS + 1 else ()

        def reply(info, xr, ktf, vtf, *rest, skip=qs[0] - chunks[c][0], qs=qs, group=group):
            if group:
                kt, vt, qx, *sent, x, terms = rest
            else:
                (x,) = rest

            @pl.when(info[0] == 0)
            def _():
                answer(xr, skip, ktf, vtf, qs, x)

            if group:

                @pl.when(info[0] > 0)
                def _():
                    for i, h in enumerate(group):
                        q = own_query(h, sent, qx)
                        terms[HP * i : HP * (i + 1), :] = score(q, head_of(kt, h), head_of(vt, h))

        ins = [info, here(got[c]), kt_far, vt_far]
        outs = [near(QR * len(qs) + tail_rows(len(qs)), LANES, bf16)]
        if group:
            ins += [kt, vt, qx, *sent]
            outs += [near(HP * len(group), R, f32)]
        res = call(reply, outs, [VM] * len(outs), ins, [SM] + [VM] * (len(ins) - 1))
        send(res[0])
        told.append(here(got[-1]))
        if group:
            own.append(here(res[1]))

    open_low = [HD * qs[0] // LANES * LANES for _, qs in answers]
    open_high = ceil_to(HD * (answers[-1][1][-1] + 1), LANES)

    def flush(info, turned, at, rows, out, ranges, sems):
        for low, high in ranges:
            for j in range(low, high, LANES):
                turn_back(turned, at, rows, j)
        for k, (low, high) in enumerate(ranges):
            write_rows(info, rows, out, low, high, sems.at[k])

    def settle_rows(rows, out, ranges, sems):
        for k, (low, high) in enumerate(ranges):
            wait_rows(rows, out, low, high, sems.at[k])

    def rest_of(info, so, kt, vt, qx, *rest):
        kvs, rest = rest[:SENDS], rest[SENDS:]
        theirs, rest = rest[: len(answers) - 2], rest[len(answers) - 2 :]
        first, second_, _, keep, out, turned, rows, held, sems = rest
        own = (first, second_)
        low = open_low[-2]

        @pl.when(info[0] == 0)
        def _():
            icopy = pltpu.make_async_copy(so, held, sems.at[0])
            ocopy = pltpu.make_async_copy(held, out, sems.at[1])
            icopy.start()
            icopy.wait()
            ocopy.start()
            ocopy.wait()

        @pl.when(info[0] > 0)
        def _():
            for c, ks in enumerate(parcels):
                for i, h in enumerate(ks):
                    block = kvs[c][block_rows * i : block_rows * (i + 1), :].astype(f32)
                    value = own_terms(own, h) + score(
                        qx[HP * (h - asked) : HP * (h - asked + 1), :],
                        padded(widen(block, 0, KB), 0.0),
                        padded(widen(block, KB, KB), 1.0),
                    )
                    turned[HD * h : HD * (h + 1), :] = value[:HD] / value[HD : HD + 1]
            for x, (_, qs) in zip(theirs, answers):
                merge(lambda h: own_terms(own, h), x, qs, turned, 0)
            ranges = [(0, low), (open_high, D)]
            flush(info, turned, 0, rows, out, ranges, sems)
            keep[...] = turned[low:open_high, :]
            settle_rows(rows, out, ranges, sems)

    ins = [info, far(stale_output), kt, vt, qx, *map(here, got[:SENDS]), *told[:-2], *own, out]
    keep, out = call(
        rest_of,
        [near(open_high - open_low[-2], R, f32), jax.ShapeDtypeStruct((N, D), bf16)],
        [VM, ANY],
        ins,
        [SM, ANY] + [VM] * (len(ins) - 3) + [ANY],
        [vm((D, R), f32), vm((R, D), bf16), vm((N, D), bf16), DMA((2,))],
        {len(ins) - 1: 1},
    )

    def join(info, keep, first, second_, theirs, _, left, out, turned, rows, sems):
        low, high = open_low[-2], open_low[-1]

        @pl.when(info[0] > 0)
        def _():
            turned[...] = keep[...]
            merge(lambda h: own_terms((first, second_), h), theirs, answers[-2][1], turned, low)
            flush(info, turned, low, rows, out, [(low, high)], sems)
            left[...] = turned[high - low :, :]
            settle_rows(rows, out, [(low, high)], sems)

    left, out = call(
        join,
        [near(open_high - open_low[-1], R, f32), jax.ShapeDtypeStruct((N, D), bf16)],
        [VM, ANY],
        [info, here(keep), *own, told[-2], out],
        [SM, VM, VM, VM, VM, ANY],
        [vm((open_high - open_low[-2], R), f32), vm((R, D), bf16), DMA((1,))],
        {5: 1},
    )

    def last(info, left, first, second_, theirs, _, out, turned, rows, sems):
        low = open_low[-1]

        @pl.when(info[0] > 0)
        def _():
            turned[...] = left[...]
            merge(lambda h: own_terms((first, second_), h), theirs, answers[-1][1], turned, low)
            flush(info, turned, low, rows, out, [(low, open_high)], sems)
            settle_rows(rows, out, [(low, open_high)], sems)

    return call(
        last,
        [jax.ShapeDtypeStruct((N, D), bf16)],
        [ANY],
        [info, here(left), *own, told[-1], out],
        [SM, VM, VM, VM, VM, ANY],
        [vm((open_high - open_low[-1], R), f32), vm((R, D), bf16), DMA((1,))],
        {5: 0},
    )[0]


def pick_plan(mesh, token_count, model_width):
    patch = mesh.shape["patch"]
    own_rows = token_count // (mesh.shape["grp"] * patch)
    own_tiles = own_rows // TILE
    fresh_tiles = own_tiles * patch // 3
    if patch != 2 or fresh_tiles > own_tiles:
        return None
    return pair_plan(H, model_width, own_rows, fresh_tiles * TILE)


def solution(mesh):
    in_specs = (
        P(("grp", "patch"), None),
        P(),
        P(),
        P(),
        P(),
        P(),
        P(("grp", "patch"), None),
        P(("grp", "patch"), None),
        P(("grp", "patch"), None),
        P("grp"),
    )
    out_specs = P(("grp", "patch"), None)

    def whole(*arrays):
        plan = pick_plan(mesh, *arrays[0].shape)
        if plan is None:
            inner = body
        else:

            def inner(*blocks):
                return pair_body(plan, *blocks)

        step = jax.shard_map(
            inner, mesh=mesh, in_specs=in_specs, out_specs=out_specs, check_vma=False
        )
        return step(*arrays)

    return whole
```

```python
import math

import jax
import jax.numpy as jnp
from jax import lax
from jax.experimental import pallas as pl
from jax.experimental.pallas import tpu as pltpu
from jax.sharding import PartitionSpec as P


H = 16
TILE = 16


epsilon = 1e-06


def modulate(row_block, shift_term, scale_term):
    values = row_block.astype(jnp.float32)
    center = values - jnp.mean(values, axis=-1, keepdims=True)
    spread = jnp.mean(center * center, axis=-1, keepdims=True)
    normed = center / jnp.sqrt(spread + epsilon)
    return (normed * (1.0 + scale_term) + shift_term).astype(jnp.bfloat16)


def head_norm(row_block, gain_vector, head_count):
    values = row_block.astype(jnp.float32).reshape(row_block.shape[0], head_count, -1)
    normed = values / jnp.sqrt(jnp.mean(values * values, axis=-1, keepdims=True) + epsilon)
    return (normed * gain_vector).astype(jnp.bfloat16).reshape(row_block.shape[0], -1)


def block_size(row_total, row_unit):
    multiple = row_total // row_unit
    chosen = 1
    for candidate in range(1, multiple + 1):
        if multiple % candidate == 0 and candidate * row_unit <= 1024:
            chosen = candidate
    return chosen * row_unit


def partial_terms(queries, key_rows, values, head_count):
    query_count = queries.shape[0]
    model_width = queries.shape[1]
    head_size = model_width // head_count
    factor = 1.0 / math.sqrt(head_size)
    query_heads = queries.reshape(query_count, head_count, head_size)
    key_heads = key_rows.reshape(key_rows.shape[0], head_count, head_size)
    value_heads = values.reshape(values.shape[0], head_count, head_size)
    scores = (
        jnp.einsum("qhd,khd->hqk", query_heads, key_heads, preferred_element_type=jnp.float32)
        * factor
    )
    weights = jnp.exp(scores)
    totals = jnp.sum(weights, axis=2).T
    numerator = jnp.einsum(
        "hqk,khd->qhd",
        weights.astype(jnp.bfloat16),
        value_heads,
        preferred_element_type=jnp.float32,
    )
    return (numerator.reshape(query_count, model_width), totals)


def own_terms(every_query, key_rows, values, head_count, row_unit):
    row_total = every_query.shape[0]
    stride = block_size(row_total, row_unit)

    def advance(turn_index, inner_sums):
        offset = turn_index * stride
        query_block = lax.dynamic_slice_in_dim(every_query, offset, stride, 0)
        numerator, totals = partial_terms(query_block, key_rows, values, head_count)
        return (
            lax.dynamic_update_slice_in_dim(inner_sums[0], numerator, offset, 0),
            lax.dynamic_update_slice_in_dim(inner_sums[1], totals, offset, 0),
        )

    starting = (
        jnp.zeros((row_total, key_rows.shape[1]), jnp.float32),
        jnp.zeros((row_total, head_count), jnp.float32),
    )
    return lax.fori_loop(0, row_total // stride, advance, starting)


def attend(queries, own_keys, own_values, head_count):
    query_count = queries.shape[0]
    model_width = queries.shape[1]
    every_query = lax.all_gather(queries, "patch", axis=0, tiled=True)
    numerator, totals = own_terms(every_query, own_keys, own_values, head_count, query_count)
    numerator, totals = (
        lax.psum_scatter(
            numerator.astype(jnp.bfloat16), "patch", scatter_dimension=0, tiled=True
        ).astype(jnp.float32),
        lax.psum_scatter(
            totals.astype(jnp.bfloat16), "patch", scatter_dimension=0, tiled=True
        ).astype(jnp.float32),
    )
    fresh_heads = numerator.reshape(query_count, head_count, -1) / totals[:, :, None]
    return fresh_heads.reshape(query_count, model_width).astype(jnp.bfloat16)


def body(
    tokens,
    projection_weight,
    shift_term,
    scale_term,
    query_gain,
    key_gain,
    stale_keys,
    stale_values,
    stale_output,
    refreshed,
):
    model_width = tokens.shape[1]
    head_count = H
    own_rows = tokens.shape[0]
    own_tiles = own_rows // TILE
    patch_count = lax.axis_size("patch")
    my_index = lax.axis_index("patch")
    share_tiles = own_tiles // 3
    most_tiles = min(own_tiles, share_tiles * patch_count)
    tile_grid = refreshed.reshape(patch_count, own_tiles)
    my_tiles = lax.dynamic_index_in_dim(tile_grid, my_index, 0, keepdims=False)
    picked = jnp.nonzero(my_tiles, size=most_tiles, fill_value=0)[0].astype(jnp.int32)
    token_tiles = tokens.reshape(own_tiles, TILE, model_width)
    chosen = token_tiles[picked].reshape(most_tiles * TILE, model_width)
    hidden = modulate(chosen, shift_term, scale_term)
    projected = jnp.dot(hidden, projection_weight, preferred_element_type=jnp.float32)
    query_new = projected[:, :model_width].astype(jnp.bfloat16)
    key_new = (
        projected[:, model_width : 2 * model_width]
        .astype(jnp.bfloat16)
        .reshape(most_tiles, TILE, model_width)
    )
    value_new = (
        projected[:, 2 * model_width :].astype(jnp.bfloat16).reshape(most_tiles, TILE, model_width)
    )
    position = jnp.maximum(jnp.cumsum(my_tiles) - 1, 0)
    fresh_tile = (my_tiles > 0)[:, None, None]
    keys_all = jnp.where(
        fresh_tile, key_new[position], stale_keys.reshape(own_tiles, TILE, model_width)
    ).reshape(own_rows, model_width)
    values_all = jnp.where(
        fresh_tile, value_new[position], stale_values.reshape(own_tiles, TILE, model_width)
    ).reshape(own_rows, model_width)
    own_keys = head_norm(keys_all, key_gain, head_count)
    queries = head_norm(query_new, query_gain, head_count)
    fresh_rows = attend(queries, own_keys, values_all, head_count)
    fresh_tiles = fresh_rows.reshape(most_tiles, TILE, model_width)
    merged = jnp.where(
        fresh_tile, fresh_tiles[position], stale_output.reshape(own_tiles, TILE, model_width)
    )
    return merged.reshape(own_rows, model_width)


LANES = 128
LAG = 3


def ceil_to(amount, unit):
    return -(-amount // unit) * unit


def pair_plan(head_count, model_width, own_rows, fresh_rows):
    head_size = model_width // head_count
    ratio = 2 * own_rows // fresh_rows
    if 2 * own_rows % fresh_rows or own_rows % LANES or fresh_rows % LANES:
        return None
    if head_size % 8 or fresh_rows // LANES * head_size % 16 or 2 * own_rows // LANES * head_size % 16:
        return None
    asked = head_count - LAG
    late = -(-(asked - LAG * ratio) // (LAG - 1))
    if not 0 < late <= ratio:
        return None
    chunks = [tuple(range(h, h + ratio)) for h in range(0, LAG * ratio, ratio)]
    chunks += [tuple(range(h, min(h + late, asked))) for h in range(LAG * ratio, asked, late)]
    return chunks, tuple(range(asked, head_count))


def pair_body(
    plan,
    tokens,
    projection_weight,
    shift_term,
    scale_term,
    query_gain,
    key_gain,
    stale_keys,
    stale_values,
    stale_output,
    refreshed,
):
    chunks, shipped = plan
    N, D = tokens.shape
    HD = query_gain.shape[0]
    heads = D // HD
    tiles = N // TILE
    R = tiles * lax.axis_size("patch") // 3 * TILE
    fresh_tiles = R // TILE
    HP = ceil_to(HD + 1, 16)
    QB, KB = R // LANES, N // LANES
    QR = QB * HD
    f32, bf16 = jnp.float32, jnp.bfloat16
    factor = math.log2(math.e) / math.sqrt(HD)
    asked = shipped[0]
    DMA = pltpu.SemaphoreType.DMA
    vm = pltpu.VMEM
    VM = pl.BlockSpec(memory_space=pltpu.VMEM)
    SM = pl.BlockSpec(memory_space=pltpu.SMEM)
    ANY = pl.BlockSpec(memory_space=pl.ANY)
    params = pltpu.CompilerParams(vmem_limit_bytes=28 * 1024 * 1024)

    def far(array):
        return pltpu.with_memory_space_constraint(array, pltpu.HBM)

    def here(array):
        return pltpu.with_memory_space_constraint(array, pltpu.VMEM)

    def near(rows, cols, dtype):
        return pltpu.VMEM((rows, cols), dtype)

    def call(kernel, outs, out_specs, ins, in_specs, scratch=(), aliases=None):
        return pl.pallas_call(
            kernel,
            out_shape=tuple(outs),
            in_specs=list(in_specs),
            out_specs=tuple(out_specs),
            scratch_shapes=list(scratch),
            input_output_aliases=aliases or {},
            compiler_params=params,
        )(*ins)

    def tail_rows(n):
        return ceil_to(2 * QB * n, 16)

    def step_rows(s):
        rows = [QR * len(chunks[s])] if s < len(chunks) else []
        if s >= LAG:
            rows.append(QR * len(chunks[s - LAG]) + tail_rows(len(chunks[s - LAG])))
        return max(rows)

    def wide(column, width):
        return jnp.concatenate([column] * (width // LANES), axis=1)

    def normed(part, gain):
        spread = jnp.mean(part * part, axis=0, keepdims=True)
        return part * lax.rsqrt(spread + epsilon) * wide(gain, part.shape[1])

    def padded(part, fill):
        extra = jnp.full((HP - HD, part.shape[1]), fill, f32)
        return jnp.concatenate([part, extra], axis=0).astype(bf16)

    def turn(source, low, high, target):
        for j in range(low, high, LANES):
            target[j - low : j - low + LANES, :] = source[:, j : j + LANES].astype(f32).T

    def pieces(parts):
        return jnp.concatenate(
            [p[:, b : b + LANES] for p in parts for b in range(0, p.shape[1], LANES)], axis=0
        ).astype(bf16)

    def widen(block, first, count):
        return jnp.concatenate(
            [block[HD * (first + b) : HD * (first + b + 1), :] for b in range(count)], axis=1
        )

    def query_of(x, i):
        return padded(widen(x[QR * i : QR * (i + 1), :].astype(f32), 0, QB), 0.0)

    def score(queries, keys, values):
        scores = lax.dot_general(
            queries, keys, (((0,), (0,)), ((), ())), preferred_element_type=f32
        )
        weights = jnp.exp2(scores * factor).astype(bf16)
        return lax.dot_general(
            values, weights, (((1,), (1,)), ((), ())), preferred_element_type=f32
        )

    def head_of(ref, h):
        return ref[HP * h : HP * (h + 1), :]

    high0 = ceil_to(HD * (chunks[0][-1] + 1), LANES)
    low1, high1 = HD * chunks[1][0] // LANES * LANES, ceil_to(HD * (chunks[1][-1] + 1), LANES)
    low2 = HD * chunks[2][0] // LANES * LANES
    lows = HD * shipped[0] // LANES * LANES

    def answer(x, kt, vt, qs, target):
        n = len(qs)
        count = tail_rows(n)
        place = lax.broadcasted_iota(jnp.int32, (count, LANES), 0)
        tail = jnp.zeros((count, LANES), f32)
        for i, h in enumerate(qs):
            terms = score(query_of(x, i), head_of(kt, h), head_of(vt, h))
            target[QR * i : QR * (i + 1), :] = pieces([terms[:HD]])
            total = terms[HD : HD + 1]
            top = total.astype(bf16).astype(f32)
            for k, piece in enumerate((top, total - top)):
                for b in range(QB):
                    row = (2 * i + k) * QB + b
                    tail = jnp.where(place == row, piece[:, LANES * b : LANES * (b + 1)], tail)
        target[QR * n : QR * n + count, :] = tail.astype(bf16)

    def total_of(tail, i):
        parts = [
            tail[(2 * i) * QB + b : (2 * i) * QB + b + 1, :]
            + tail[(2 * i + 1) * QB + b : (2 * i + 1) * QB + b + 1, :]
            for b in range(QB)
        ]
        return jnp.concatenate(parts, axis=1)

    bounds = (0, 3 * heads // 8, 5 * heads // 8, 7 * heads // 8, heads)
    groups = [tuple(range(a, b)) for a, b in zip(bounds, bounds[1:])]

    def own_terms(own, h):
        g = [h in group for group in groups].index(True)
        i = h - groups[g][0]
        return own[g][HP * i : HP * (i + 1), :]

    def own_query(h, sent, stash, qx):
        if h >= asked:
            return qx[HP * (h - asked) : HP * (h - asked + 1), :]
        c = [h in qs for qs in chunks].index(True)
        if c < LAG:
            return query_of(sent[c], h - chunks[c][0])
        return query_of(stash, h - chunks[LAG][0])

    def settle(info, new, mix):
        for i in range(fresh_tiles):
            mix[pl.ds(pl.multiple_of(info[1 + i], TILE), TILE), :] = new[TILE * i : TILE * (i + 1), :]

    def merge(own_terms, x, qs, target, low):
        tail = x[QR * len(qs) : QR * len(qs) + tail_rows(len(qs)), :].astype(f32)
        for i, h in enumerate(qs):
            terms = own_terms(h)
            theirs = widen(x[QR * i : QR * (i + 1), :].astype(f32), 0, QB)
            target[HD * h - low : HD * (h + 1) - low, :] = (terms[:HD] + theirs) / (
                terms[HD : HD + 1] + total_of(tail, i)
            )

    def write_rows(info, rows, out, low, high, sem):
        if low == high:
            return
        for i in range(fresh_tiles):
            pltpu.make_async_copy(
                rows.at[TILE * i : TILE * (i + 1), low:high],
                out.at[pl.ds(pl.multiple_of(info[1 + i], TILE), TILE), low:high],
                sem,
            ).start()

    def wait_rows(rows, out, low, high, sem):
        if low == high:
            return
        pltpu.make_async_copy(rows.at[:, low:high], out.at[0:R, low:high], sem).wait()

    def turn_back(turned, low, rows, j):
        rows[:, j : j + LANES] = turned[j - low : j - low + LANES, :].T.astype(bf16)

    block_rows = 2 * KB * HD

    def front(
        flags, tok, w, shift, scale, gq, gk, sk, sv,
        info, gains, hid, wq, x0, kv,
        fl, sh, sc, g0, g1, tbuf, kbuf, vbuf, qt, st, sems,
    ):
        def load(source, target, k):
            copy = pltpu.make_async_copy(source, target, sems.at[k])
            copy.start()
            return copy

        cflags = load(flags, fl, 0)
        cg0 = load(gq, g0, 1)
        cg1 = load(gk, g1, 2)
        ck = load(sk.at[:, lows:D], kbuf, 3)
        cv = load(sv.at[:, lows:D], vbuf, 4)
        ctok = load(tok, tbuf, 5)
        cshift = load(shift, sh, 6)
        cscale = load(scale, sc, 7)
        cw = load(w.at[:, 0:high0], wq.at[:, 0:high0], 8)
        cflags.wait()
        me = lax.axis_index("patch")
        base = me * tiles

        def note(t, seen):
            info[1 + seen] = t * TILE
            return seen + fl[base + t]

        count = lax.fori_loop(0, tiles, note, 0)
        info[0] = count
        rest = pltpu.make_async_copy(w.at[:, high0:high1], wq.at[:, high0:high1], sems.at[9])

        @pl.when(count > 0)
        def _():
            rest.start()

        cg0.wait()
        cg1.wait()
        eye = lax.broadcasted_iota(jnp.int32, (HD, HD), 0) == lax.broadcasted_iota(
            jnp.int32, (HD, HD), 1
        )
        for k, g in enumerate((g0, g1)):
            row = jnp.broadcast_to(g[...].reshape(1, HD), (HD, HD))
            column = jnp.sum(jnp.where(eye, row, 0.0), axis=1, keepdims=True)
            gains[HD * k : HD * (k + 1), :] = jnp.broadcast_to(column, (HD, LANES))
        ck.wait()
        cv.wait()

        @pl.when(count == 0)
        def _():
            turn(kbuf, 0, D - lows, st.at[0])
            turn(vbuf, 0, D - lows, st.at[1])
            gain = gains[HD : 2 * HD, :]
            for i, h in enumerate(shipped):
                at = HD * h - lows
                block = pieces([normed(st[0, at : at + HD, :], gain), st[1, at : at + HD, :]])
                if i == 0:
                    x0[...] = block
                else:
                    kv[block_rows * (i - 1) : block_rows * i, :] = block

        cshift.wait()
        cscale.wait()
        ctok.wait()

        @pl.when(count > 0)
        def _():
            up = 1.0 + sc[...].reshape(1, D)
            down = sh[...].reshape(1, D)
            for i in range(fresh_tiles):
                x = tbuf[pl.ds(pl.multiple_of(info[1 + i], TILE), TILE), :].astype(f32)
                center = x - jnp.mean(x, axis=1, keepdims=True)
                spread = jnp.mean(center * center, axis=1, keepdims=True)
                hid[TILE * i : TILE * (i + 1), :] = (
                    center * lax.rsqrt(spread + epsilon) * up + down
                ).astype(bf16)

        cw.wait()

        @pl.when(count > 0)
        def _():
            projected = jnp.dot(hid[...], wq[:, 0:high0], preferred_element_type=f32).astype(bf16)
            turn(projected, 0, high0, qt)
            gain = gains[0:HD, :]
            for i, h in enumerate(chunks[0]):
                x0[QR * i : QR * (i + 1), :] = pieces([normed(qt[HD * h : HD * (h + 1), :], gain)])
            rest.wait()

    info, gains, hidden, wq, x0, kv = call(
        front,
        [
            pltpu.SMEM((fresh_tiles + 2,), jnp.int32),
            near(2 * HD, LANES, f32),
            near(R, D, bf16),
            near(D, high1, bf16),
            near(QR * len(chunks[0]), LANES, bf16),
            near(block_rows * (LAG - 1), LANES, bf16),
        ],
        [SM] + [VM] * 5,
        [
            far(a)
            for a in (
                refreshed, tokens, projection_weight, shift_term, scale_term,
                query_gain, key_gain, stale_keys, stale_values,
            )
        ],
        [ANY] * 9,
        [
            pltpu.SMEM(refreshed.shape, jnp.int32),
            vm(shift_term.shape, f32),
            vm(scale_term.shape, f32),
            vm(query_gain.shape, f32),
            vm(key_gain.shape, f32),
            vm((N, D), bf16),
            vm((N, D - lows), bf16),
            vm((N, D - lows), bf16),
            vm((high0, R), f32),
            vm((2, D - lows, N), f32),
            DMA((10,)),
        ],
    )

    late_weight = here(lax.optimization_barrier((projection_weight, x0))[0])
    info = pltpu.with_memory_space_constraint(info, pltpu.SMEM)
    gains, hidden, wq = here(gains), here(hidden), here(wq)
    got = []

    def send(array):
        got.append(lax.ppermute(array, "patch", [(0, 1), (1, 0)]))

    send(x0)

    def following(
        info, gains, hid, wq, sk, sv, kv, x1, kt, vbuf, qt, kbuf, turned, sems
    ):
        @pl.when(info[0] > 0)
        def _():
            projected = jnp.dot(hid[...], wq[:, low1:high1], preferred_element_type=f32).astype(bf16)
            turn(projected, 0, high1 - low1, qt)
            gain = gains[0:HD, :]
            for i, h in enumerate(chunks[1]):
                part = normed(qt[HD * h - low1 : HD * (h + 1) - low1, :], gain)
                x1[QR * i : QR * (i + 1), :] = pieces([part])

        @pl.when(info[0] == 0)
        def _():
            width = ceil_to(HD * asked, LANES)
            kcopy = pltpu.make_async_copy(sk.at[:, 0:width], kbuf.at[:, 0:width], sems.at[0])
            vcopy = pltpu.make_async_copy(sv.at[:, 0:width], vbuf.at[:, 0:width], sems.at[1])
            kcopy.start()
            vcopy.start()
            x1[...] = kv[0:block_rows, :]
            gain = gains[HD : 2 * HD, :]
            kcopy.wait()
            turn(kbuf, 0, width, turned)
            for h in range(asked):
                kt[HP * h : HP * (h + 1), :] = padded(normed(turned[HD * h : HD * (h + 1), :], gain), 0.0)
            vcopy.wait()

    kv = here(kv)
    x1, kt_far, v_far = call(
        following,
        [near(step_rows(1), LANES, bf16), near(HP * asked, N, bf16), near(N, D, bf16)],
        [VM] * 3,
        [info, gains, hidden, wq, far(stale_keys), far(stale_values), kv],
        [SM, VM, VM, VM, ANY, ANY, VM],
        [vm((high1 - low1, R), f32), vm((N, D), bf16), vm((D, N), f32), DMA((2,))],
    )
    kt_far, v_far = here(kt_far), here(v_far)
    send(x1)

    def second(info, gains, hid, w, kv, v_far, x2, stash, qx, vt, qt, turned):
        @pl.when(info[0] > 0)
        def _():
            projected = jnp.dot(hid[...], w[:, low2:D], preferred_element_type=f32).astype(bf16)
            turn(projected, 0, D - low2, qt)
            gain = gains[0:HD, :]
            for h in range(chunks[2][0], heads):
                part = normed(qt[HD * h - low2 : HD * (h + 1) - low2, :], gain)
                if h in chunks[2]:
                    i = h - chunks[2][0]
                    x2[QR * i : QR * (i + 1), :] = pieces([part])
                elif h < asked:
                    i = h - chunks[LAG][0]
                    stash[QR * i : QR * (i + 1), :] = pieces([part])
                else:
                    i = h - asked
                    qx[HP * i : HP * (i + 1), :] = padded(part, 0.0)

        @pl.when(info[0] == 0)
        def _():
            x2[...] = kv[block_rows : 2 * block_rows, :]
            turn(v_far, 0, ceil_to(HD * asked, LANES), turned)
            for h in range(asked):
                vt[HP * h : HP * (h + 1), :] = padded(turned[HD * h : HD * (h + 1), :], 1.0)

    x2, stash, qx, vt_far = call(
        second,
        [
            near(step_rows(2), LANES, bf16),
            near(QR * (asked - chunks[LAG][0]), LANES, bf16),
            near(HP * len(shipped), R, bf16),
            near(HP * asked, N, bf16),
        ],
        [VM] * 4,
        [info, gains, hidden, late_weight, kv, v_far],
        [SM] + [VM] * 5,
        [vm((D - low2, R), f32), vm((D, N), f32)],
    )
    stash, qx, vt_far = here(stash), here(qx), here(vt_far)
    send(x2)
    sent = [here(x0), here(x1), here(x2)]

    def third(info, hid, w, sk, turned, new, mix, sem):
        @pl.when(info[0] > 0)
        def _():
            kcopy = pltpu.make_async_copy(sk, mix, sem)
            kcopy.start()
            new[...] = jnp.dot(hid[...], w[:, D : 2 * D], preferred_element_type=f32).astype(bf16)
            kcopy.wait()
            settle(info, new, mix)
            turn(mix, 0, D, turned)

    (keys_turned,) = call(
        third,
        [near(D, N, f32)],
        [VM],
        [info, hidden, late_weight, far(stale_keys)],
        [SM, VM, VM, ANY],
        [vm((R, D), bf16), vm((N, D), bf16), DMA],
    )
    keys_turned = here(keys_turned)

    own, told = [], []
    kt = vt = vnew = vall = held = out = None
    project_at, turn_at = 1, 2

    for c, qs in enumerate(chunks):
        s = c + LAG
        after = chunks[s] if s < len(chunks) else ()
        group = groups[c - turn_at] if c >= turn_at else ()

        def reply(info, xr, ktf, vtf, stash, *rest, c=c, qs=qs, after=after, group=group):
            if c == project_at:
                gains, keys_turned, hid, w, sv, so, x, vnew, kt, vall, held, sems = rest
            elif c == turn_at:
                kt, qx, *sent, vnew, vall, held, x, terms, vt, out, mix, turned, sem = rest
            elif group:
                kt, vt, qx, *sent, x, terms = rest
            else:
                (x,) = rest

            @pl.when(info[0] == 0)
            def _():
                answer(xr, ktf, vtf, qs, x)

            @pl.when(info[0] > 0)
            def _():
                if after:
                    at = QR * (after[0] - chunks[LAG][0])
                    x[0 : QR * len(after), :] = stash[at : at + QR * len(after), :]
                if c == project_at:
                    vcopy = pltpu.make_async_copy(sv, vall, sems.at[0])
                    vcopy.start()
                    ocopy = pltpu.make_async_copy(so, held, sems.at[1])
                    ocopy.start()
                    vnew[...] = jnp.dot(hid[...], w[:, 2 * D :], preferred_element_type=f32).astype(bf16)
                    gain = gains[HD : 2 * HD, :]
                    for h in range(heads):
                        part = normed(keys_turned[HD * h : HD * (h + 1), :], gain)
                        kt[HP * h : HP * (h + 1), :] = padded(part, 0.0)
                    vcopy.wait()
                    ocopy.wait()
                if c == turn_at:
                    ocopy = pltpu.make_async_copy(held, out, sem)
                    ocopy.start()
                    mix[...] = vall[...]
                    settle(info, vnew, mix)
                    turn(mix, 0, D, turned)
                    for h in range(heads):
                        vt[HP * h : HP * (h + 1), :] = padded(turned[HD * h : HD * (h + 1), :], 1.0)
                for i, h in enumerate(group):
                    q = own_query(h, sent, stash, qx)
                    terms[HP * i : HP * (i + 1), :] = score(q, head_of(kt, h), head_of(vt, h))
                if c == turn_at:
                    ocopy.wait()

        ins = [info, here(got[c]), kt_far, vt_far, stash]
        outs = [near(step_rows(s), LANES, bf16)]
        given = [VM] * len(ins[1:])
        spaces = [VM]
        scratch = []
        if c == project_at:
            ins += [gains, keys_turned, hidden, late_weight, far(stale_values), far(stale_output)]
            given += [VM] * 4 + [ANY] * 2
            outs += [near(R, D, bf16), near(HP * heads, N, bf16), near(N, D, bf16), near(N, D, bf16)]
            spaces += [VM] * 4
            scratch = [DMA((2,))]
        elif c == turn_at:
            ins += [kt, qx, *sent, vnew, vall, held]
            given += [VM] * (5 + len(sent))
            outs += [near(HP * len(group), R, f32), near(HP * heads, N, bf16), jax.ShapeDtypeStruct((N, D), bf16)]
            spaces += [VM, VM, ANY]
            scratch = [vm((N, D), bf16), vm((D, N), f32), DMA]
        elif group:
            ins += [kt, vt, qx, *sent]
            given += [VM] * (3 + len(sent))
            outs += [near(HP * len(group), R, f32)]
            spaces += [VM]
        res = call(reply, outs, spaces, ins, [SM] + given, scratch)
        send(res[0])
        told.append(here(got[-1]))
        if c == project_at:
            vnew, kt, vall, held = map(here, res[1:])
        elif group:
            own.append(here(res[1]))
            if c == turn_at:
                vt, out = here(res[2]), res[3]

    answers = chunks

    open_low = [HD * qs[0] // LANES * LANES for qs in answers]
    open_high = ceil_to(HD * (answers[-1][-1] + 1), LANES)

    def flush(info, turned, at, rows, out, ranges, sems):
        for low, high in ranges:
            for j in range(low, high, LANES):
                turn_back(turned, at, rows, j)
        for k, (low, high) in enumerate(ranges):
            write_rows(info, rows, out, low, high, sems.at[k])

    def settle_rows(rows, out, ranges, sems):
        for k, (low, high) in enumerate(ranges):
            wait_rows(rows, out, low, high, sems.at[k])

    def rest_of(info, so, kt, vt, qx, stash, *rest):
        sent, rest = rest[:LAG], rest[LAG:]
        kvs, rest = rest[:LAG], rest[LAG:]
        theirs, rest = rest[: len(answers) - 2], rest[len(answers) - 2 :]
        early, rest = rest[: len(groups) - 1], rest[len(groups) - 1 :]
        _, terms, keep, out, turned, rows, held, sems = rest
        own = (*early, terms)
        low = open_low[-2]

        @pl.when(info[0] == 0)
        def _():
            icopy = pltpu.make_async_copy(so, held, sems.at[0])
            ocopy = pltpu.make_async_copy(held, out, sems.at[1])
            icopy.start()
            icopy.wait()
            ocopy.start()
            ocopy.wait()

        @pl.when(info[0] > 0)
        def _():
            for i, h in enumerate(groups[-1]):
                q = own_query(h, sent, stash, qx)
                terms[HP * i : HP * (i + 1), :] = score(q, head_of(kt, h), head_of(vt, h))
            for i, h in enumerate(shipped):
                block = kvs[i][...].astype(f32)
                value = own_terms(own, h) + score(
                    qx[HP * i : HP * (i + 1), :],
                    padded(widen(block, 0, KB), 0.0),
                    padded(widen(block, KB, KB), 1.0),
                )
                turned[HD * h : HD * (h + 1), :] = value[:HD] / value[HD : HD + 1]
            for x, qs in zip(theirs, answers):
                merge(lambda h: own_terms(own, h), x, qs, turned, 0)
            ranges = [(0, low), (open_high, D)]
            flush(info, turned, 0, rows, out, ranges, sems)
            keep[...] = turned[low:open_high, :]
            settle_rows(rows, out, ranges, sems)

    ins = [
        info, far(stale_output), kt, vt, qx, stash, *sent,
        *map(here, got[:LAG]), *told[:-2], *own, out,
    ]
    terms, keep, out = call(
        rest_of,
        [
            near(HP * len(groups[-1]), R, f32),
            near(open_high - open_low[-2], R, f32),
            jax.ShapeDtypeStruct((N, D), bf16),
        ],
        [VM, VM, ANY],
        ins,
        [SM, ANY] + [VM] * (len(ins) - 3) + [ANY],
        [vm((D, R), f32), vm((R, D), bf16), vm((N, D), bf16), DMA((2,))],
        {len(ins) - 1: 2},
    )
    own.append(here(terms))

    def join(info, keep, theirs, *rest):
        own, (_, left, out, turned, rows, sems) = rest[: len(groups)], rest[len(groups) :]
        low, high = open_low[-2], open_low[-1]

        @pl.when(info[0] > 0)
        def _():
            turned[...] = keep[...]
            merge(lambda h: own_terms(own, h), theirs, answers[-2], turned, low)
            flush(info, turned, low, rows, out, [(low, high)], sems)
            left[...] = turned[high - low :, :]
            settle_rows(rows, out, [(low, high)], sems)

    left, out = call(
        join,
        [near(open_high - open_low[-1], R, f32), jax.ShapeDtypeStruct((N, D), bf16)],
        [VM, ANY],
        [info, here(keep), told[-2], *own, out],
        [SM, VM, VM] + [VM] * len(own) + [ANY],
        [vm((open_high - open_low[-2], R), f32), vm((R, D), bf16), DMA((1,))],
        {3 + len(own): 1},
    )

    def last(info, left, theirs, *rest):
        own, (_, out, turned, rows, sems) = rest[: len(groups)], rest[len(groups) :]
        low = open_low[-1]

        @pl.when(info[0] > 0)
        def _():
            turned[...] = left[...]
            merge(lambda h: own_terms(own, h), theirs, answers[-1], turned, low)
            flush(info, turned, low, rows, out, [(low, open_high)], sems)
            settle_rows(rows, out, [(low, open_high)], sems)

    return call(
        last,
        [jax.ShapeDtypeStruct((N, D), bf16)],
        [ANY],
        [info, here(left), told[-1], *own, out],
        [SM, VM, VM] + [VM] * len(own) + [ANY],
        [vm((open_high - open_low[-1], R), f32), vm((R, D), bf16), DMA((1,))],
        {3 + len(own): 0},
    )[0]


def pick_plan(mesh, token_count, model_width):
    patch = mesh.shape["patch"]
    own_rows = token_count // (mesh.shape["grp"] * patch)
    own_tiles = own_rows // TILE
    fresh_tiles = own_tiles * patch // 3
    if patch != 2 or fresh_tiles > own_tiles:
        return None
    return pair_plan(H, model_width, own_rows, fresh_tiles * TILE)


def solution(mesh):
    in_specs = (
        P(("grp", "patch"), None),
        P(),
        P(),
        P(),
        P(),
        P(),
        P(("grp", "patch"), None),
        P(("grp", "patch"), None),
        P(("grp", "patch"), None),
        P("grp"),
    )
    out_specs = P(("grp", "patch"), None)

    def whole(*arrays):
        plan = pick_plan(mesh, *arrays[0].shape)
        if plan is None:
            inner = body
        else:

            def inner(*blocks):
                return pair_body(plan, *blocks)

        step = jax.shard_map(
            inner, mesh=mesh, in_specs=in_specs, out_specs=out_specs, check_vma=False
        )
        return step(*arrays)

    return whole
```

```python
import math

import jax
import jax.numpy as jnp
from jax import lax
from jax.experimental import pallas as pl
from jax.experimental.pallas import tpu as pltpu
from jax.sharding import PartitionSpec as P


H = 16
TILE = 16


epsilon = 1e-06


def modulate(row_block, shift_term, scale_term):
    values = row_block.astype(jnp.float32)
    center = values - jnp.mean(values, axis=-1, keepdims=True)
    spread = jnp.mean(center * center, axis=-1, keepdims=True)
    normed = center / jnp.sqrt(spread + epsilon)
    return (normed * (1.0 + scale_term) + shift_term).astype(jnp.bfloat16)


def head_norm(row_block, gain_vector, head_count):
    values = row_block.astype(jnp.float32).reshape(row_block.shape[0], head_count, -1)
    normed = values / jnp.sqrt(jnp.mean(values * values, axis=-1, keepdims=True) + epsilon)
    return (normed * gain_vector).astype(jnp.bfloat16).reshape(row_block.shape[0], -1)


def block_size(row_total, row_unit):
    multiple = row_total // row_unit
    chosen = 1
    for candidate in range(1, multiple + 1):
        if multiple % candidate == 0 and candidate * row_unit <= 1024:
            chosen = candidate
    return chosen * row_unit


def partial_terms(queries, key_rows, values, head_count):
    query_count = queries.shape[0]
    model_width = queries.shape[1]
    head_size = model_width // head_count
    factor = 1.0 / math.sqrt(head_size)
    query_heads = queries.reshape(query_count, head_count, head_size)
    key_heads = key_rows.reshape(key_rows.shape[0], head_count, head_size)
    value_heads = values.reshape(values.shape[0], head_count, head_size)
    scores = (
        jnp.einsum("qhd,khd->hqk", query_heads, key_heads, preferred_element_type=jnp.float32)
        * factor
    )
    weights = jnp.exp(scores)
    totals = jnp.sum(weights, axis=2).T
    numerator = jnp.einsum(
        "hqk,khd->qhd",
        weights.astype(jnp.bfloat16),
        value_heads,
        preferred_element_type=jnp.float32,
    )
    return (numerator.reshape(query_count, model_width), totals)


def own_terms(every_query, key_rows, values, head_count, row_unit):
    row_total = every_query.shape[0]
    stride = block_size(row_total, row_unit)

    def advance(turn_index, inner_sums):
        offset = turn_index * stride
        query_block = lax.dynamic_slice_in_dim(every_query, offset, stride, 0)
        numerator, totals = partial_terms(query_block, key_rows, values, head_count)
        return (
            lax.dynamic_update_slice_in_dim(inner_sums[0], numerator, offset, 0),
            lax.dynamic_update_slice_in_dim(inner_sums[1], totals, offset, 0),
        )

    starting = (
        jnp.zeros((row_total, key_rows.shape[1]), jnp.float32),
        jnp.zeros((row_total, head_count), jnp.float32),
    )
    return lax.fori_loop(0, row_total // stride, advance, starting)


def attend(queries, own_keys, own_values, head_count):
    query_count = queries.shape[0]
    model_width = queries.shape[1]
    every_query = lax.all_gather(queries, "patch", axis=0, tiled=True)
    numerator, totals = own_terms(every_query, own_keys, own_values, head_count, query_count)
    numerator, totals = (
        lax.psum_scatter(
            numerator.astype(jnp.bfloat16), "patch", scatter_dimension=0, tiled=True
        ).astype(jnp.float32),
        lax.psum_scatter(
            totals.astype(jnp.bfloat16), "patch", scatter_dimension=0, tiled=True
        ).astype(jnp.float32),
    )
    fresh_heads = numerator.reshape(query_count, head_count, -1) / totals[:, :, None]
    return fresh_heads.reshape(query_count, model_width).astype(jnp.bfloat16)


def body(
    tokens,
    projection_weight,
    shift_term,
    scale_term,
    query_gain,
    key_gain,
    stale_keys,
    stale_values,
    stale_output,
    refreshed,
):
    model_width = tokens.shape[1]
    head_count = H
    own_rows = tokens.shape[0]
    own_tiles = own_rows // TILE
    patch_count = lax.axis_size("patch")
    my_index = lax.axis_index("patch")
    share_tiles = own_tiles // 3
    most_tiles = min(own_tiles, share_tiles * patch_count)
    tile_grid = refreshed.reshape(patch_count, own_tiles)
    my_tiles = lax.dynamic_index_in_dim(tile_grid, my_index, 0, keepdims=False)
    picked = jnp.nonzero(my_tiles, size=most_tiles, fill_value=0)[0].astype(jnp.int32)
    token_tiles = tokens.reshape(own_tiles, TILE, model_width)
    chosen = token_tiles[picked].reshape(most_tiles * TILE, model_width)
    hidden = modulate(chosen, shift_term, scale_term)
    projected = jnp.dot(hidden, projection_weight, preferred_element_type=jnp.float32)
    query_new = projected[:, :model_width].astype(jnp.bfloat16)
    key_new = (
        projected[:, model_width : 2 * model_width]
        .astype(jnp.bfloat16)
        .reshape(most_tiles, TILE, model_width)
    )
    value_new = (
        projected[:, 2 * model_width :].astype(jnp.bfloat16).reshape(most_tiles, TILE, model_width)
    )
    position = jnp.maximum(jnp.cumsum(my_tiles) - 1, 0)
    fresh_tile = (my_tiles > 0)[:, None, None]
    keys_all = jnp.where(
        fresh_tile, key_new[position], stale_keys.reshape(own_tiles, TILE, model_width)
    ).reshape(own_rows, model_width)
    values_all = jnp.where(
        fresh_tile, value_new[position], stale_values.reshape(own_tiles, TILE, model_width)
    ).reshape(own_rows, model_width)
    own_keys = head_norm(keys_all, key_gain, head_count)
    queries = head_norm(query_new, query_gain, head_count)
    fresh_rows = attend(queries, own_keys, values_all, head_count)
    fresh_tiles = fresh_rows.reshape(most_tiles, TILE, model_width)
    merged = jnp.where(
        fresh_tile, fresh_tiles[position], stale_output.reshape(own_tiles, TILE, model_width)
    )
    return merged.reshape(own_rows, model_width)


LANES = 128
LAG = 3


def ceil_to(amount, unit):
    return -(-amount // unit) * unit


def pair_plan(head_count, model_width, own_rows, fresh_rows):
    head_size = model_width // head_count
    ratio = 2 * own_rows // fresh_rows
    if 2 * own_rows % fresh_rows or own_rows % LANES or fresh_rows % LANES:
        return None
    if head_size % 8 or fresh_rows // LANES * head_size % 16 or 2 * own_rows // LANES * head_size % 16:
        return None
    asked = head_count - LAG
    late = min(ratio, asked - LAG * ratio - 1)
    if not 0 < late <= ratio:
        return None
    chunks = [tuple(range(h, h + ratio)) for h in range(0, LAG * ratio, ratio)]
    chunks += [tuple(range(h, min(h + late, asked))) for h in range(LAG * ratio, asked, late)]
    return chunks, tuple(range(asked, head_count))


def pair_body(
    plan,
    tokens,
    projection_weight,
    shift_term,
    scale_term,
    query_gain,
    key_gain,
    stale_keys,
    stale_values,
    stale_output,
    refreshed,
):
    chunks, shipped = plan
    N, D = tokens.shape
    HD = query_gain.shape[0]
    heads = D // HD
    tiles = N // TILE
    R = tiles * lax.axis_size("patch") // 3 * TILE
    fresh_tiles = R // TILE
    HP = ceil_to(HD + 1, 16)
    QB, KB = R // LANES, N // LANES
    QR = QB * HD
    f32, bf16 = jnp.float32, jnp.bfloat16
    factor = math.log2(math.e) / math.sqrt(HD)
    asked = shipped[0]
    DMA = pltpu.SemaphoreType.DMA
    vm = pltpu.VMEM
    VM = pl.BlockSpec(memory_space=pltpu.VMEM)
    SM = pl.BlockSpec(memory_space=pltpu.SMEM)
    ANY = pl.BlockSpec(memory_space=pl.ANY)
    params = pltpu.CompilerParams(vmem_limit_bytes=28 * 1024 * 1024)

    def far(array):
        return pltpu.with_memory_space_constraint(array, pltpu.HBM)

    def here(array):
        return pltpu.with_memory_space_constraint(array, pltpu.VMEM)

    def near(rows, cols, dtype):
        return pltpu.VMEM((rows, cols), dtype)

    def call(kernel, outs, out_specs, ins, in_specs, scratch=(), aliases=None):
        return pl.pallas_call(
            kernel,
            out_shape=tuple(outs),
            in_specs=list(in_specs),
            out_specs=tuple(out_specs),
            scratch_shapes=list(scratch),
            input_output_aliases=aliases or {},
            compiler_params=params,
        )(*ins)

    def tail_rows(n):
        return ceil_to(QB * n, 8)

    def step_rows(s):
        rows = [QR * len(chunks[s])] if s < len(chunks) else []
        if s >= LAG:
            rows.append(QR * len(chunks[s - LAG]) + tail_rows(len(chunks[s - LAG])))
        return max(rows)

    def wide(column, width):
        return jnp.concatenate([column] * (width // LANES), axis=1)

    def normed(part, gain):
        spread = jnp.mean(part * part, axis=0, keepdims=True)
        return part * lax.rsqrt(spread + epsilon) * wide(gain, part.shape[1])

    def padded(part, fill):
        extra = jnp.full((HP - HD, part.shape[1]), fill, f32)
        return jnp.concatenate([part, extra], axis=0).astype(bf16)

    def turn(source, low, high, target):
        for j in range(low, high, LANES):
            target[j - low : j - low + LANES, :] = source[:, j : j + LANES].astype(f32).T

    def pieces(parts):
        return jnp.concatenate(
            [p[:, b : b + LANES] for p in parts for b in range(0, p.shape[1], LANES)], axis=0
        ).astype(bf16)

    def widen(block, first, count):
        return jnp.concatenate(
            [block[HD * (first + b) : HD * (first + b + 1), :] for b in range(count)], axis=1
        )

    def query_of(x, i):
        return padded(widen(x[QR * i : QR * (i + 1), :].astype(f32), 0, QB), 0.0)

    def score(queries, keys, values):
        scores = lax.dot_general(
            queries, keys, (((0,), (0,)), ((), ())), preferred_element_type=f32
        )
        weights = jnp.exp2(scores * factor).astype(bf16)
        return lax.dot_general(
            values, weights, (((1,), (1,)), ((), ())), preferred_element_type=f32
        )

    def head_of(ref, h):
        return ref[HP * h : HP * (h + 1), :]

    high0 = ceil_to(HD * (chunks[0][-1] + 1), LANES)
    low1, high1 = HD * chunks[1][0] // LANES * LANES, ceil_to(HD * (chunks[1][-1] + 1), LANES)
    low2 = HD * chunks[2][0] // LANES * LANES
    lows = HD * shipped[0] // LANES * LANES

    def answer(x, kt, vt, qs, target):
        n = len(qs)
        count = tail_rows(n)
        place = lax.broadcasted_iota(jnp.int32, (count, LANES), 0)
        tail = jnp.zeros((count, LANES), f32)
        for i, h in enumerate(qs):
            terms = score(query_of(x, i), head_of(kt, h), head_of(vt, h))
            target[QR * i : QR * (i + 1), :] = pieces([terms[:HD]])
            total = terms[HD : HD + 1]
            for b in range(QB):
                tail = jnp.where(place == QB * i + b, total[:, LANES * b : LANES * (b + 1)], tail)
        target[QR * n : QR * n + count, :] = tail.astype(bf16)

    def total_of(tail, i):
        return jnp.concatenate([tail[QB * i + b : QB * i + b + 1, :] for b in range(QB)], axis=1)

    bounds = (0, 7 * heads // 16, 3 * heads // 4, 7 * heads // 8, heads)
    groups = [tuple(range(a, b)) for a, b in zip(bounds, bounds[1:])]

    def own_terms(own, h):
        g = [h in group for group in groups].index(True)
        i = h - groups[g][0]
        return own[g][HP * i : HP * (i + 1), :]

    def own_query(h, sent, stash, qx):
        if h >= asked:
            return qx[HP * (h - asked) : HP * (h - asked + 1), :]
        c = [h in qs for qs in chunks].index(True)
        if c < LAG:
            return query_of(sent[c], h - chunks[c][0])
        return query_of(stash, h - chunks[LAG][0])

    def settle(info, new, mix):
        for i in range(fresh_tiles):
            mix[pl.ds(pl.multiple_of(info[1 + i], TILE), TILE), :] = new[TILE * i : TILE * (i + 1), :]

    def merge(own_terms, x, qs, target, low):
        tail = x[QR * len(qs) : QR * len(qs) + tail_rows(len(qs)), :].astype(f32)
        for i, h in enumerate(qs):
            terms = own_terms(h)
            theirs = widen(x[QR * i : QR * (i + 1), :].astype(f32), 0, QB)
            target[HD * h - low : HD * (h + 1) - low, :] = (terms[:HD] + theirs) / (
                terms[HD : HD + 1] + total_of(tail, i)
            )

    def write_rows(info, rows, out, low, high, sem):
        if low == high:
            return
        for i in range(fresh_tiles):
            pltpu.make_async_copy(
                rows.at[TILE * i : TILE * (i + 1), low:high],
                out.at[pl.ds(pl.multiple_of(info[1 + i], TILE), TILE), low:high],
                sem,
            ).start()

    def wait_rows(rows, out, low, high, sem):
        if low == high:
            return
        pltpu.make_async_copy(rows.at[:, low:high], out.at[0:R, low:high], sem).wait()

    def turn_back(turned, low, rows, j):
        rows[:, j : j + LANES] = turned[j - low : j - low + LANES, :].T.astype(bf16)

    block_rows = 2 * KB * HD

    def front(
        flags, tok, w, shift, scale, gq, gk, sk, sv,
        info, gains, hid, wq, x0, kv,
        fl, sh, sc, g0, g1, tbuf, kbuf, vbuf, qt, st, sems,
    ):
        def load(source, target, k):
            copy = pltpu.make_async_copy(source, target, sems.at[k])
            copy.start()
            return copy

        cflags = load(flags, fl, 0)
        cg0 = load(gq, g0, 1)
        cg1 = load(gk, g1, 2)
        ck = load(sk.at[:, lows:D], kbuf, 3)
        cv = load(sv.at[:, lows:D], vbuf, 4)
        ctok = load(tok, tbuf, 5)
        cshift = load(shift, sh, 6)
        cscale = load(scale, sc, 7)
        cw = load(w.at[:, 0:high0], wq.at[:, 0:high0], 8)
        cflags.wait()
        me = lax.axis_index("patch")
        base = me * tiles

        def note(t, seen):
            info[1 + seen] = t * TILE
            return seen + fl[base + t]

        count = lax.fori_loop(0, tiles, note, 0)
        info[0] = count
        rest = pltpu.make_async_copy(w.at[:, high0:high1], wq.at[:, high0:high1], sems.at[9])

        @pl.when(count > 0)
        def _():
            rest.start()

        cg0.wait()
        cg1.wait()
        eye = lax.broadcasted_iota(jnp.int32, (HD, HD), 0) == lax.broadcasted_iota(
            jnp.int32, (HD, HD), 1
        )
        for k, g in enumerate((g0, g1)):
            row = jnp.broadcast_to(g[...].reshape(1, HD), (HD, HD))
            column = jnp.sum(jnp.where(eye, row, 0.0), axis=1, keepdims=True)
            gains[HD * k : HD * (k + 1), :] = jnp.broadcast_to(column, (HD, LANES))
        ck.wait()
        cv.wait()

        @pl.when(count == 0)
        def _():
            turn(kbuf, 0, D - lows, st.at[0])
            turn(vbuf, 0, D - lows, st.at[1])
            gain = gains[HD : 2 * HD, :]
            for i, h in enumerate(shipped):
                at = HD * h - lows
                block = pieces([normed(st[0, at : at + HD, :], gain), st[1, at : at + HD, :]])
                if i == 0:
                    x0[...] = block
                else:
                    kv[block_rows * (i - 1) : block_rows * i, :] = block

        cshift.wait()
        cscale.wait()
        ctok.wait()

        @pl.when(count > 0)
        def _():
            up = 1.0 + sc[...].reshape(1, D)
            down = sh[...].reshape(1, D)
            for i in range(fresh_tiles):
                x = tbuf[pl.ds(pl.multiple_of(info[1 + i], TILE), TILE), :].astype(f32)
                center = x - jnp.mean(x, axis=1, keepdims=True)
                spread = jnp.mean(center * center, axis=1, keepdims=True)
                hid[TILE * i : TILE * (i + 1), :] = (
                    center * lax.rsqrt(spread + epsilon) * up + down
                ).astype(bf16)

        cw.wait()

        @pl.when(count > 0)
        def _():
            projected = jnp.dot(hid[...], wq[:, 0:high0], preferred_element_type=f32).astype(bf16)
            turn(projected, 0, high0, qt)
            gain = gains[0:HD, :]
            for i, h in enumerate(chunks[0]):
                x0[QR * i : QR * (i + 1), :] = pieces([normed(qt[HD * h : HD * (h + 1), :], gain)])
            rest.wait()

    info, gains, hidden, wq, x0, kv = call(
        front,
        [
            pltpu.SMEM((fresh_tiles + 2,), jnp.int32),
            near(2 * HD, LANES, f32),
            near(R, D, bf16),
            near(D, high1, bf16),
            near(QR * len(chunks[0]), LANES, bf16),
            near(block_rows * (LAG - 1), LANES, bf16),
        ],
        [SM] + [VM] * 5,
        [
            far(a)
            for a in (
                refreshed, tokens, projection_weight, shift_term, scale_term,
                query_gain, key_gain, stale_keys, stale_values,
            )
        ],
        [ANY] * 9,
        [
            pltpu.SMEM(refreshed.shape, jnp.int32),
            vm(shift_term.shape, f32),
            vm(scale_term.shape, f32),
            vm(query_gain.shape, f32),
            vm(key_gain.shape, f32),
            vm((N, D), bf16),
            vm((N, D - lows), bf16),
            vm((N, D - lows), bf16),
            vm((high0, R), f32),
            vm((2, D - lows, N), f32),
            DMA((10,)),
        ],
    )

    late_weight = here(lax.optimization_barrier((projection_weight, x0))[0])
    info = pltpu.with_memory_space_constraint(info, pltpu.SMEM)
    gains, hidden, wq = here(gains), here(hidden), here(wq)
    got = []

    def send(array):
        got.append(lax.ppermute(array, "patch", [(0, 1), (1, 0)]))

    send(x0)

    def following(
        info, gains, hid, wq, sk, sv, kv, x1, kt, vbuf, qt, kbuf, turned, sems
    ):
        @pl.when(info[0] > 0)
        def _():
            projected = jnp.dot(hid[...], wq[:, low1:high1], preferred_element_type=f32).astype(bf16)
            turn(projected, 0, high1 - low1, qt)
            gain = gains[0:HD, :]
            for i, h in enumerate(chunks[1]):
                part = normed(qt[HD * h - low1 : HD * (h + 1) - low1, :], gain)
                x1[QR * i : QR * (i + 1), :] = pieces([part])

        @pl.when(info[0] == 0)
        def _():
            width = ceil_to(HD * asked, LANES)
            kcopy = pltpu.make_async_copy(sk.at[:, 0:width], kbuf.at[:, 0:width], sems.at[0])
            vcopy = pltpu.make_async_copy(sv.at[:, 0:width], vbuf.at[:, 0:width], sems.at[1])
            kcopy.start()
            vcopy.start()
            x1[...] = kv[0:block_rows, :]
            gain = gains[HD : 2 * HD, :]
            kcopy.wait()
            turn(kbuf, 0, width, turned)
            for h in range(asked):
                kt[HP * h : HP * (h + 1), :] = padded(normed(turned[HD * h : HD * (h + 1), :], gain), 0.0)
            vcopy.wait()

    kv = here(kv)
    x1, kt_far, v_far = call(
        following,
        [near(step_rows(1), LANES, bf16), near(HP * asked, N, bf16), near(N, D, bf16)],
        [VM] * 3,
        [info, gains, hidden, wq, far(stale_keys), far(stale_values), kv],
        [SM, VM, VM, VM, ANY, ANY, VM],
        [vm((high1 - low1, R), f32), vm((N, D), bf16), vm((D, N), f32), DMA((2,))],
    )
    kt_far, v_far = here(kt_far), here(v_far)
    send(x1)

    def second(info, gains, hid, w, kv, v_far, x2, stash, qx, vt, qt, turned):
        @pl.when(info[0] > 0)
        def _():
            projected = jnp.dot(hid[...], w[:, low2:D], preferred_element_type=f32).astype(bf16)
            turn(projected, 0, D - low2, qt)
            gain = gains[0:HD, :]
            for h in range(chunks[2][0], heads):
                part = normed(qt[HD * h - low2 : HD * (h + 1) - low2, :], gain)
                if h in chunks[2]:
                    i = h - chunks[2][0]
                    x2[QR * i : QR * (i + 1), :] = pieces([part])
                elif h < asked:
                    i = h - chunks[LAG][0]
                    stash[QR * i : QR * (i + 1), :] = pieces([part])
                else:
                    i = h - asked
                    qx[HP * i : HP * (i + 1), :] = padded(part, 0.0)

        @pl.when(info[0] == 0)
        def _():
            x2[...] = kv[block_rows : 2 * block_rows, :]
            turn(v_far, 0, ceil_to(HD * asked, LANES), turned)
            for h in range(asked):
                vt[HP * h : HP * (h + 1), :] = padded(turned[HD * h : HD * (h + 1), :], 1.0)

    x2, stash, qx, vt_far = call(
        second,
        [
            near(step_rows(2), LANES, bf16),
            near(QR * (asked - chunks[LAG][0]), LANES, bf16),
            near(HP * len(shipped), R, bf16),
            near(HP * asked, N, bf16),
        ],
        [VM] * 4,
        [info, gains, hidden, late_weight, kv, v_far],
        [SM] + [VM] * 5,
        [vm((D - low2, R), f32), vm((D, N), f32)],
    )
    stash, qx, vt_far = here(stash), here(qx), here(vt_far)
    send(x2)
    sent = [here(x0), here(x1), here(x2)]

    def third(info, hid, w, sk, turned, new, mix, sem):
        @pl.when(info[0] > 0)
        def _():
            kcopy = pltpu.make_async_copy(sk, mix, sem)
            kcopy.start()
            new[...] = jnp.dot(hid[...], w[:, D : 2 * D], preferred_element_type=f32).astype(bf16)
            kcopy.wait()
            settle(info, new, mix)
            turn(mix, 0, D, turned)

    (keys_turned,) = call(
        third,
        [near(D, N, f32)],
        [VM],
        [info, hidden, late_weight, far(stale_keys)],
        [SM, VM, VM, ANY],
        [vm((R, D), bf16), vm((N, D), bf16), DMA],
    )
    keys_turned = here(keys_turned)

    own, told = [], []
    kt = vt = vnew = vall = held = out = None
    project_at, turn_at = 1, 2

    for c, qs in enumerate(chunks):
        s = c + LAG
        after = chunks[s] if s < len(chunks) else ()
        group = groups[c - turn_at] if c >= turn_at else ()

        def reply(info, xr, ktf, vtf, stash, *rest, c=c, qs=qs, after=after, group=group):
            if c == project_at:
                hid, w, sv, so, x, vnew, vall, held, sems = rest
            elif c == turn_at:
                gains, keys_turned, qx, *sent, vnew, vall, held, x, terms, kt, vt, out, mix, turned, sem = rest
            elif group:
                kt, vt, qx, *sent, x, terms = rest
            else:
                (x,) = rest

            @pl.when(info[0] == 0)
            def _():
                answer(xr, ktf, vtf, qs, x)

            @pl.when(info[0] > 0)
            def _():
                if after:
                    at = QR * (after[0] - chunks[LAG][0])
                    x[0 : QR * len(after), :] = stash[at : at + QR * len(after), :]
                if c == project_at:
                    vcopy = pltpu.make_async_copy(sv, vall, sems.at[0])
                    vcopy.start()
                    ocopy = pltpu.make_async_copy(so, held, sems.at[1])
                    ocopy.start()
                    vnew[...] = jnp.dot(hid[...], w[:, 2 * D :], preferred_element_type=f32).astype(bf16)
                    vcopy.wait()
                    ocopy.wait()
                if c == turn_at:
                    ocopy = pltpu.make_async_copy(held, out, sem)
                    ocopy.start()
                    gain = gains[HD : 2 * HD, :]
                    for h in range(heads):
                        part = normed(keys_turned[HD * h : HD * (h + 1), :], gain)
                        kt[HP * h : HP * (h + 1), :] = padded(part, 0.0)
                    mix[...] = vall[...]
                    settle(info, vnew, mix)
                    turn(mix, 0, D, turned)
                    for h in range(heads):
                        vt[HP * h : HP * (h + 1), :] = padded(turned[HD * h : HD * (h + 1), :], 1.0)
                for i, h in enumerate(group):
                    q = own_query(h, sent, stash, qx)
                    terms[HP * i : HP * (i + 1), :] = score(q, head_of(kt, h), head_of(vt, h))
                if c == turn_at:
                    ocopy.wait()

        ins = [info, here(got[c]), kt_far, vt_far, stash]
        outs = [near(step_rows(s), LANES, bf16)]
        given = [VM] * len(ins[1:])
        spaces = [VM]
        scratch = []
        if c == project_at:
            ins += [hidden, late_weight, far(stale_values), far(stale_output)]
            given += [VM] * 2 + [ANY] * 2
            outs += [near(R, D, bf16), near(N, D, bf16), near(N, D, bf16)]
            spaces += [VM] * 3
            scratch = [DMA((2,))]
        elif c == turn_at:
            ins += [gains, keys_turned, qx, *sent, vnew, vall, held]
            given += [VM] * (6 + len(sent))
            outs += [near(HP * len(group), R, f32)] + [near(HP * heads, N, bf16)] * 2
            outs += [jax.ShapeDtypeStruct((N, D), bf16)]
            spaces += [VM] * 3 + [ANY]
            scratch = [vm((N, D), bf16), vm((D, N), f32), DMA]
        elif group:
            ins += [kt, vt, qx, *sent]
            given += [VM] * (3 + len(sent))
            outs += [near(HP * len(group), R, f32)]
            spaces += [VM]
        res = call(reply, outs, spaces, ins, [SM] + given, scratch)
        send(res[0])
        told.append(here(got[-1]))
        if c == project_at:
            vnew, vall, held = map(here, res[1:])
        elif group:
            own.append(here(res[1]))
            if c == turn_at:
                kt, vt, out = here(res[2]), here(res[3]), res[4]

    answers = chunks

    open_low = [HD * qs[0] // LANES * LANES for qs in answers]
    open_high = ceil_to(HD * (answers[-1][-1] + 1), LANES)

    def flush(info, turned, at, rows, out, ranges, sems):
        for low, high in ranges:
            for j in range(low, high, LANES):
                turn_back(turned, at, rows, j)
        for k, (low, high) in enumerate(ranges):
            write_rows(info, rows, out, low, high, sems.at[k])

    def settle_rows(rows, out, ranges, sems):
        for k, (low, high) in enumerate(ranges):
            wait_rows(rows, out, low, high, sems.at[k])

    def rest_of(info, so, kt, vt, qx, stash, *rest):
        sent, rest = rest[:LAG], rest[LAG:]
        kvs, rest = rest[:LAG], rest[LAG:]
        theirs, rest = rest[: len(answers) - 2], rest[len(answers) - 2 :]
        early, rest = rest[: len(groups) - 1], rest[len(groups) - 1 :]
        _, terms, keep, out, turned, rows, held, sems = rest
        own = (*early, terms)
        low = open_low[-2]

        @pl.when(info[0] == 0)
        def _():
            icopy = pltpu.make_async_copy(so, held, sems.at[0])
            ocopy = pltpu.make_async_copy(held, out, sems.at[1])
            icopy.start()
            icopy.wait()
            ocopy.start()
            ocopy.wait()

        @pl.when(info[0] > 0)
        def _():
            for i, h in enumerate(groups[-1]):
                q = own_query(h, sent, stash, qx)
                terms[HP * i : HP * (i + 1), :] = score(q, head_of(kt, h), head_of(vt, h))
            for i, h in enumerate(shipped):
                block = kvs[i][...].astype(f32)
                value = own_terms(own, h) + score(
                    qx[HP * i : HP * (i + 1), :],
                    padded(widen(block, 0, KB), 0.0),
                    padded(widen(block, KB, KB), 1.0),
                )
                turned[HD * h : HD * (h + 1), :] = value[:HD] / value[HD : HD + 1]
            for x, qs in zip(theirs, answers):
                merge(lambda h: own_terms(own, h), x, qs, turned, 0)
            ranges = [(0, low), (open_high, D)]
            flush(info, turned, 0, rows, out, ranges, sems)
            keep[...] = turned[low:open_high, :]
            settle_rows(rows, out, ranges, sems)

    ins = [
        info, far(stale_output), kt, vt, qx, stash, *sent,
        *map(here, got[:LAG]), *told[:-2], *own, out,
    ]
    terms, keep, out = call(
        rest_of,
        [
            near(HP * len(groups[-1]), R, f32),
            near(open_high - open_low[-2], R, f32),
            jax.ShapeDtypeStruct((N, D), bf16),
        ],
        [VM, VM, ANY],
        ins,
        [SM, ANY] + [VM] * (len(ins) - 3) + [ANY],
        [vm((D, R), f32), vm((R, D), bf16), vm((N, D), bf16), DMA((2,))],
        {len(ins) - 1: 2},
    )
    own.append(here(terms))

    def last(info, keep, theirs, latest, *rest):
        own, (_, out, turned, rows, sems) = rest[: len(groups)], rest[len(groups) :]
        low = open_low[-2]

        @pl.when(info[0] > 0)
        def _():
            turned[...] = keep[...]
            merge(lambda h: own_terms(own, h), theirs, answers[-2], turned, low)
            merge(lambda h: own_terms(own, h), latest, answers[-1], turned, low)
            flush(info, turned, low, rows, out, [(low, open_high)], sems)
            settle_rows(rows, out, [(low, open_high)], sems)

    return call(
        last,
        [jax.ShapeDtypeStruct((N, D), bf16)],
        [ANY],
        [info, here(keep), *told[-2:], *own, out],
        [SM, VM, VM, VM] + [VM] * len(own) + [ANY],
        [vm((open_high - open_low[-2], R), f32), vm((R, D), bf16), DMA((1,))],
        {4 + len(own): 0},
    )[0]


def pick_plan(mesh, token_count, model_width):
    patch = mesh.shape["patch"]
    own_rows = token_count // (mesh.shape["grp"] * patch)
    own_tiles = own_rows // TILE
    fresh_tiles = own_tiles * patch // 3
    if patch != 2 or fresh_tiles > own_tiles:
        return None
    return pair_plan(H, model_width, own_rows, fresh_tiles * TILE)


def solution(mesh):
    in_specs = (
        P(("grp", "patch"), None),
        P(),
        P(),
        P(),
        P(),
        P(),
        P(("grp", "patch"), None),
        P(("grp", "patch"), None),
        P(("grp", "patch"), None),
        P("grp"),
    )
    out_specs = P(("grp", "patch"), None)

    def whole(*arrays):
        plan = pick_plan(mesh, *arrays[0].shape)
        if plan is None:
            inner = body
        else:

            def inner(*blocks):
                return pair_body(plan, *blocks)

        step = jax.shard_map(
            inner, mesh=mesh, in_specs=in_specs, out_specs=out_specs, check_vma=False
        )
        return step(*arrays)

    return whole
```

```python
import math

import jax
import jax.numpy as jnp
from jax import lax
from jax.experimental import pallas as pl
from jax.experimental.pallas import tpu as pltpu
from jax.sharding import PartitionSpec as P


H = 16
TILE = 16


epsilon = 1e-06


def modulate(row_block, shift_term, scale_term):
    values = row_block.astype(jnp.float32)
    center = values - jnp.mean(values, axis=-1, keepdims=True)
    spread = jnp.mean(center * center, axis=-1, keepdims=True)
    normed = center / jnp.sqrt(spread + epsilon)
    return (normed * (1.0 + scale_term) + shift_term).astype(jnp.bfloat16)


def head_norm(row_block, gain_vector, head_count):
    values = row_block.astype(jnp.float32).reshape(row_block.shape[0], head_count, -1)
    normed = values / jnp.sqrt(jnp.mean(values * values, axis=-1, keepdims=True) + epsilon)
    return (normed * gain_vector).astype(jnp.bfloat16).reshape(row_block.shape[0], -1)


def block_size(row_total, row_unit):
    multiple = row_total // row_unit
    chosen = 1
    for candidate in range(1, multiple + 1):
        if multiple % candidate == 0 and candidate * row_unit <= 1024:
            chosen = candidate
    return chosen * row_unit


def partial_terms(queries, key_rows, values, head_count):
    query_count = queries.shape[0]
    model_width = queries.shape[1]
    head_size = model_width // head_count
    factor = 1.0 / math.sqrt(head_size)
    query_heads = queries.reshape(query_count, head_count, head_size)
    key_heads = key_rows.reshape(key_rows.shape[0], head_count, head_size)
    value_heads = values.reshape(values.shape[0], head_count, head_size)
    scores = (
        jnp.einsum("qhd,khd->hqk", query_heads, key_heads, preferred_element_type=jnp.float32)
        * factor
    )
    weights = jnp.exp(scores)
    totals = jnp.sum(weights, axis=2).T
    numerator = jnp.einsum(
        "hqk,khd->qhd",
        weights.astype(jnp.bfloat16),
        value_heads,
        preferred_element_type=jnp.float32,
    )
    return (numerator.reshape(query_count, model_width), totals)


def own_terms(every_query, key_rows, values, head_count, row_unit):
    row_total = every_query.shape[0]
    stride = block_size(row_total, row_unit)

    def advance(turn_index, inner_sums):
        offset = turn_index * stride
        query_block = lax.dynamic_slice_in_dim(every_query, offset, stride, 0)
        numerator, totals = partial_terms(query_block, key_rows, values, head_count)
        return (
            lax.dynamic_update_slice_in_dim(inner_sums[0], numerator, offset, 0),
            lax.dynamic_update_slice_in_dim(inner_sums[1], totals, offset, 0),
        )

    starting = (
        jnp.zeros((row_total, key_rows.shape[1]), jnp.float32),
        jnp.zeros((row_total, head_count), jnp.float32),
    )
    return lax.fori_loop(0, row_total // stride, advance, starting)


def attend(queries, own_keys, own_values, head_count):
    query_count = queries.shape[0]
    model_width = queries.shape[1]
    every_query = lax.all_gather(queries, "patch", axis=0, tiled=True)
    numerator, totals = own_terms(every_query, own_keys, own_values, head_count, query_count)
    numerator, totals = (
        lax.psum_scatter(
            numerator.astype(jnp.bfloat16), "patch", scatter_dimension=0, tiled=True
        ).astype(jnp.float32),
        lax.psum_scatter(
            totals.astype(jnp.bfloat16), "patch", scatter_dimension=0, tiled=True
        ).astype(jnp.float32),
    )
    fresh_heads = numerator.reshape(query_count, head_count, -1) / totals[:, :, None]
    return fresh_heads.reshape(query_count, model_width).astype(jnp.bfloat16)


def body(
    tokens,
    projection_weight,
    shift_term,
    scale_term,
    query_gain,
    key_gain,
    stale_keys,
    stale_values,
    stale_output,
    refreshed,
):
    model_width = tokens.shape[1]
    head_count = H
    own_rows = tokens.shape[0]
    own_tiles = own_rows // TILE
    patch_count = lax.axis_size("patch")
    my_index = lax.axis_index("patch")
    share_tiles = own_tiles // 3
    most_tiles = min(own_tiles, share_tiles * patch_count)
    tile_grid = refreshed.reshape(patch_count, own_tiles)
    my_tiles = lax.dynamic_index_in_dim(tile_grid, my_index, 0, keepdims=False)
    picked = jnp.nonzero(my_tiles, size=most_tiles, fill_value=0)[0].astype(jnp.int32)
    token_tiles = tokens.reshape(own_tiles, TILE, model_width)
    chosen = token_tiles[picked].reshape(most_tiles * TILE, model_width)
    hidden = modulate(chosen, shift_term, scale_term)
    projected = jnp.dot(hidden, projection_weight, preferred_element_type=jnp.float32)
    query_new = projected[:, :model_width].astype(jnp.bfloat16)
    key_new = (
        projected[:, model_width : 2 * model_width]
        .astype(jnp.bfloat16)
        .reshape(most_tiles, TILE, model_width)
    )
    value_new = (
        projected[:, 2 * model_width :].astype(jnp.bfloat16).reshape(most_tiles, TILE, model_width)
    )
    position = jnp.maximum(jnp.cumsum(my_tiles) - 1, 0)
    fresh_tile = (my_tiles > 0)[:, None, None]
    keys_all = jnp.where(
        fresh_tile, key_new[position], stale_keys.reshape(own_tiles, TILE, model_width)
    ).reshape(own_rows, model_width)
    values_all = jnp.where(
        fresh_tile, value_new[position], stale_values.reshape(own_tiles, TILE, model_width)
    ).reshape(own_rows, model_width)
    own_keys = head_norm(keys_all, key_gain, head_count)
    queries = head_norm(query_new, query_gain, head_count)
    fresh_rows = attend(queries, own_keys, values_all, head_count)
    fresh_tiles = fresh_rows.reshape(most_tiles, TILE, model_width)
    merged = jnp.where(
        fresh_tile, fresh_tiles[position], stale_output.reshape(own_tiles, TILE, model_width)
    )
    return merged.reshape(own_rows, model_width)


LANES = 128
LAG = 3


def ceil_to(amount, unit):
    return -(-amount // unit) * unit


def pair_plan(head_count, model_width, own_rows, fresh_rows):
    head_size = model_width // head_count
    ratio = 2 * own_rows // fresh_rows
    if 2 * own_rows % fresh_rows or own_rows % LANES or fresh_rows % LANES:
        return None
    if head_size % 8 or fresh_rows // LANES * head_size % 16 or 2 * own_rows // LANES * head_size % 16:
        return None
    asked = head_count - LAG
    late = min(ratio, asked - LAG * ratio - 1)
    if not 0 < late <= ratio:
        return None
    chunks = [tuple(range(h, h + ratio)) for h in range(0, LAG * ratio, ratio)]
    chunks += [tuple(range(h, min(h + late, asked))) for h in range(LAG * ratio, asked, late)]
    return chunks, tuple(range(asked, head_count))


def pair_body(
    plan,
    tokens,
    projection_weight,
    shift_term,
    scale_term,
    query_gain,
    key_gain,
    stale_keys,
    stale_values,
    stale_output,
    refreshed,
):
    chunks, shipped = plan
    N, D = tokens.shape
    HD = query_gain.shape[0]
    heads = D // HD
    tiles = N // TILE
    R = tiles * lax.axis_size("patch") // 3 * TILE
    fresh_tiles = R // TILE
    HP = ceil_to(HD + 1, 16)
    QB, KB = R // LANES, N // LANES
    QR = QB * HD
    f32, bf16 = jnp.float32, jnp.bfloat16
    factor = math.log2(math.e) / math.sqrt(HD)
    asked = shipped[0]
    DMA = pltpu.SemaphoreType.DMA
    vm = pltpu.VMEM
    VM = pl.BlockSpec(memory_space=pltpu.VMEM)
    SM = pl.BlockSpec(memory_space=pltpu.SMEM)
    ANY = pl.BlockSpec(memory_space=pl.ANY)
    params = pltpu.CompilerParams(vmem_limit_bytes=28 * 1024 * 1024)

    def far(array):
        return pltpu.with_memory_space_constraint(array, pltpu.HBM)

    def here(array):
        return pltpu.with_memory_space_constraint(array, pltpu.VMEM)

    def near(rows, cols, dtype):
        return pltpu.VMEM((rows, cols), dtype)

    def call(kernel, outs, out_specs, ins, in_specs, scratch=(), aliases=None):
        return pl.pallas_call(
            kernel,
            out_shape=tuple(outs),
            in_specs=list(in_specs),
            out_specs=tuple(out_specs),
            scratch_shapes=list(scratch),
            input_output_aliases=aliases or {},
            compiler_params=params,
        )(*ins)

    def tail_rows(n):
        return ceil_to(QB * n, 8)

    def step_rows(s):
        rows = [QR * len(chunks[s])] if s < len(chunks) else []
        if s >= LAG:
            rows.append(QR * len(chunks[s - LAG]) + tail_rows(len(chunks[s - LAG])))
        return max(rows)

    def wide(column, width):
        return jnp.concatenate([column] * (width // LANES), axis=1)

    def normed(part, gain):
        spread = jnp.mean(part * part, axis=0, keepdims=True)
        return part * lax.rsqrt(spread + epsilon) * wide(gain, part.shape[1])

    def padded(part, fill):
        extra = jnp.full((HP - HD, part.shape[1]), fill, f32)
        return jnp.concatenate([part, extra], axis=0).astype(bf16)

    def turn(source, low, high, target):
        for j in range(low, high, LANES):
            target[j - low : j - low + LANES, :] = source[:, j : j + LANES].astype(f32).T

    def pieces(parts):
        return jnp.concatenate(
            [p[:, b : b + LANES] for p in parts for b in range(0, p.shape[1], LANES)], axis=0
        ).astype(bf16)

    def widen(block, first, count):
        return jnp.concatenate(
            [block[HD * (first + b) : HD * (first + b + 1), :] for b in range(count)], axis=1
        )

    def query_of(x, i):
        return padded(widen(x[QR * i : QR * (i + 1), :].astype(f32), 0, QB), 0.0)

    def score(queries, keys, values):
        scores = lax.dot_general(
            queries, keys, (((0,), (0,)), ((), ())), preferred_element_type=f32
        )
        weights = jnp.exp2(scores * factor).astype(bf16)
        return lax.dot_general(
            values, weights, (((1,), (1,)), ((), ())), preferred_element_type=f32
        )

    def head_of(ref, h):
        return ref[HP * h : HP * (h + 1), :]

    high0 = ceil_to(HD * (chunks[0][-1] + 1), LANES)
    low1, high1 = HD * chunks[1][0] // LANES * LANES, ceil_to(HD * (chunks[1][-1] + 1), LANES)
    low2 = HD * chunks[2][0] // LANES * LANES
    lows = HD * shipped[0] // LANES * LANES

    def answer(x, kt, vt, qs, target):
        n = len(qs)
        count = tail_rows(n)
        place = lax.broadcasted_iota(jnp.int32, (count, LANES), 0)
        tail = jnp.zeros((count, LANES), f32)
        for i, h in enumerate(qs):
            terms = score(query_of(x, i), head_of(kt, h), head_of(vt, h))
            target[QR * i : QR * (i + 1), :] = pieces([terms[:HD]])
            total = terms[HD : HD + 1]
            for b in range(QB):
                tail = jnp.where(place == QB * i + b, total[:, LANES * b : LANES * (b + 1)], tail)
        target[QR * n : QR * n + count, :] = tail.astype(bf16)

    def total_of(tail, i):
        return jnp.concatenate([tail[QB * i + b : QB * i + b + 1, :] for b in range(QB)], axis=1)

    bounds = (0, 7 * heads // 16, 3 * heads // 4, 7 * heads // 8, heads)
    groups = [tuple(range(a, b)) for a, b in zip(bounds, bounds[1:])]

    def own_terms(own, h):
        g = [h in group for group in groups].index(True)
        i = h - groups[g][0]
        return own[g][HP * i : HP * (i + 1), :]

    def own_query(h, sent, stash, qx):
        if h >= asked:
            return qx[HP * (h - asked) : HP * (h - asked + 1), :]
        c = [h in qs for qs in chunks].index(True)
        if c < LAG:
            return query_of(sent[c], h - chunks[c][0])
        return query_of(stash, h - chunks[LAG][0])

    def settle(info, new, mix):
        for i in range(fresh_tiles):
            mix[pl.ds(pl.multiple_of(info[1 + i], TILE), TILE), :] = new[TILE * i : TILE * (i + 1), :]

    def merge(own_terms, x, qs, target, low):
        tail = x[QR * len(qs) : QR * len(qs) + tail_rows(len(qs)), :].astype(f32)
        for i, h in enumerate(qs):
            terms = own_terms(h)
            theirs = widen(x[QR * i : QR * (i + 1), :].astype(f32), 0, QB)
            target[HD * h - low : HD * (h + 1) - low, :] = (terms[:HD] + theirs) / (
                terms[HD : HD + 1] + total_of(tail, i)
            )

    def write_rows(info, rows, out, low, high, sem):
        if low == high:
            return
        for i in range(fresh_tiles):
            pltpu.make_async_copy(
                rows.at[TILE * i : TILE * (i + 1), low:high],
                out.at[pl.ds(pl.multiple_of(info[1 + i], TILE), TILE), low:high],
                sem,
            ).start()

    def wait_rows(rows, out, low, high, sem):
        if low == high:
            return
        pltpu.make_async_copy(rows.at[:, low:high], out.at[0:R, low:high], sem).wait()

    def turn_back(turned, low, rows, j):
        rows[:, j : j + LANES] = turned[j - low : j - low + LANES, :].T.astype(bf16)

    def parcel(st, gains, i):
        at = HD * shipped[i] - lows
        key = normed(st[0, at : at + HD, :], gains[HD : 2 * HD, :])
        return pieces([key, st[1, at : at + HD, :]])

    def front(
        flags, tok, w, shift, scale, gq, gk, sk, sv,
        info, gains, hid, wq, x0, st,
        fl, sh, sc, g0, g1, tbuf, kbuf, vbuf, qt, sems,
    ):
        def load(source, target, k):
            copy = pltpu.make_async_copy(source, target, sems.at[k])
            copy.start()
            return copy

        cflags = load(flags, fl, 0)
        cg0 = load(gq, g0, 1)
        cg1 = load(gk, g1, 2)
        ck = load(sk.at[:, lows:D], kbuf, 3)
        cv = load(sv.at[:, lows:D], vbuf, 4)
        ctok = load(tok, tbuf, 5)
        cshift = load(shift, sh, 6)
        cscale = load(scale, sc, 7)
        cw = load(w.at[:, 0:high0], wq.at[:, 0:high0], 8)
        cflags.wait()
        me = lax.axis_index("patch")
        base = me * tiles

        def note(t, seen):
            info[1 + seen] = t * TILE
            return seen + fl[base + t]

        count = lax.fori_loop(0, tiles, note, 0)
        info[0] = count
        rest = pltpu.make_async_copy(w.at[:, high0:high1], wq.at[:, high0:high1], sems.at[9])

        @pl.when(count > 0)
        def _():
            rest.start()

        cg0.wait()
        cg1.wait()
        eye = lax.broadcasted_iota(jnp.int32, (HD, HD), 0) == lax.broadcasted_iota(
            jnp.int32, (HD, HD), 1
        )
        for k, g in enumerate((g0, g1)):
            row = jnp.broadcast_to(g[...].reshape(1, HD), (HD, HD))
            column = jnp.sum(jnp.where(eye, row, 0.0), axis=1, keepdims=True)
            gains[HD * k : HD * (k + 1), :] = jnp.broadcast_to(column, (HD, LANES))
        ck.wait()
        cv.wait()

        @pl.when(count == 0)
        def _():
            turn(kbuf, 0, D - lows, st.at[0])
            turn(vbuf, 0, D - lows, st.at[1])
            x0[...] = parcel(st, gains, 0)

        cshift.wait()
        cscale.wait()
        ctok.wait()

        @pl.when(count > 0)
        def _():
            up = 1.0 + sc[...].reshape(1, D)
            down = sh[...].reshape(1, D)
            for i in range(fresh_tiles):
                x = tbuf[pl.ds(pl.multiple_of(info[1 + i], TILE), TILE), :].astype(f32)
                center = x - jnp.mean(x, axis=1, keepdims=True)
                spread = jnp.mean(center * center, axis=1, keepdims=True)
                hid[TILE * i : TILE * (i + 1), :] = (
                    center * lax.rsqrt(spread + epsilon) * up + down
                ).astype(bf16)

        cw.wait()

        @pl.when(count > 0)
        def _():
            projected = jnp.dot(hid[...], wq[:, 0:high0], preferred_element_type=f32).astype(bf16)
            turn(projected, 0, high0, qt)
            gain = gains[0:HD, :]
            for i, h in enumerate(chunks[0]):
                x0[QR * i : QR * (i + 1), :] = pieces([normed(qt[HD * h : HD * (h + 1), :], gain)])
            rest.wait()

    info, gains, hidden, wq, x0, kv = call(
        front,
        [
            pltpu.SMEM((fresh_tiles + 2,), jnp.int32),
            near(2 * HD, LANES, f32),
            near(R, D, bf16),
            near(D, high1, bf16),
            near(QR * len(chunks[0]), LANES, bf16),
            pltpu.VMEM((2, D - lows, N), f32),
        ],
        [SM] + [VM] * 5,
        [
            far(a)
            for a in (
                refreshed, tokens, projection_weight, shift_term, scale_term,
                query_gain, key_gain, stale_keys, stale_values,
            )
        ],
        [ANY] * 9,
        [
            pltpu.SMEM(refreshed.shape, jnp.int32),
            vm(shift_term.shape, f32),
            vm(scale_term.shape, f32),
            vm(query_gain.shape, f32),
            vm(key_gain.shape, f32),
            vm((N, D), bf16),
            vm((N, D - lows), bf16),
            vm((N, D - lows), bf16),
            vm((high0, R), f32),
            DMA((10,)),
        ],
    )

    late_weight = here(lax.optimization_barrier((projection_weight, x0))[0])
    info = pltpu.with_memory_space_constraint(info, pltpu.SMEM)
    gains, hidden, wq = here(gains), here(hidden), here(wq)
    got = []

    def send(array):
        got.append(lax.ppermute(array, "patch", [(0, 1), (1, 0)]))

    send(x0)

    def following(
        info, gains, hid, wq, sk, sv, kv, x1, kt, vbuf, qt, kbuf, turned, sems
    ):
        @pl.when(info[0] > 0)
        def _():
            projected = jnp.dot(hid[...], wq[:, low1:high1], preferred_element_type=f32).astype(bf16)
            turn(projected, 0, high1 - low1, qt)
            gain = gains[0:HD, :]
            for i, h in enumerate(chunks[1]):
                part = normed(qt[HD * h - low1 : HD * (h + 1) - low1, :], gain)
                x1[QR * i : QR * (i + 1), :] = pieces([part])

        @pl.when(info[0] == 0)
        def _():
            width = ceil_to(HD * asked, LANES)
            kcopy = pltpu.make_async_copy(sk.at[:, 0:width], kbuf.at[:, 0:width], sems.at[0])
            vcopy = pltpu.make_async_copy(sv.at[:, 0:width], vbuf.at[:, 0:width], sems.at[1])
            kcopy.start()
            vcopy.start()
            x1[...] = parcel(kv, gains, 1)
            gain = gains[HD : 2 * HD, :]
            kcopy.wait()
            turn(kbuf, 0, width, turned)
            for h in range(asked):
                kt[HP * h : HP * (h + 1), :] = padded(normed(turned[HD * h : HD * (h + 1), :], gain), 0.0)
            vcopy.wait()

    kv = here(kv)
    x1, kt_far, v_far = call(
        following,
        [near(step_rows(1), LANES, bf16), near(HP * asked, N, bf16), near(N, D, bf16)],
        [VM] * 3,
        [info, gains, hidden, wq, far(stale_keys), far(stale_values), kv],
        [SM, VM, VM, VM, ANY, ANY, VM],
        [vm((high1 - low1, R), f32), vm((N, D), bf16), vm((D, N), f32), DMA((2,))],
    )
    kt_far, v_far = here(kt_far), here(v_far)
    send(x1)

    def second(info, gains, hid, w, kv, v_far, x2, stash, qx, vt, qt, turned):
        @pl.when(info[0] > 0)
        def _():
            projected = jnp.dot(hid[...], w[:, low2:D], preferred_element_type=f32).astype(bf16)
            turn(projected, 0, D - low2, qt)
            gain = gains[0:HD, :]
            for h in range(chunks[2][0], heads):
                part = normed(qt[HD * h - low2 : HD * (h + 1) - low2, :], gain)
                if h in chunks[2]:
                    i = h - chunks[2][0]
                    x2[QR * i : QR * (i + 1), :] = pieces([part])
                elif h < asked:
                    i = h - chunks[LAG][0]
                    stash[QR * i : QR * (i + 1), :] = pieces([part])
                else:
                    i = h - asked
                    qx[HP * i : HP * (i + 1), :] = padded(part, 0.0)

        @pl.when(info[0] == 0)
        def _():
            x2[...] = parcel(kv, gains, 2)
            turn(v_far, 0, ceil_to(HD * asked, LANES), turned)
            for h in range(asked):
                vt[HP * h : HP * (h + 1), :] = padded(turned[HD * h : HD * (h + 1), :], 1.0)

    x2, stash, qx, vt_far = call(
        second,
        [
            near(step_rows(2), LANES, bf16),
            near(QR * (asked - chunks[LAG][0]), LANES, bf16),
            near(HP * len(shipped), R, bf16),
            near(HP * asked, N, bf16),
        ],
        [VM] * 4,
        [info, gains, hidden, late_weight, kv, v_far],
        [SM] + [VM] * 5,
        [vm((D - low2, R), f32), vm((D, N), f32)],
    )
    stash, qx, vt_far = here(stash), here(qx), here(vt_far)
    send(x2)
    sent = [here(x0), here(x1), here(x2)]

    def third(info, hid, w, sk, turned, new, mix, sem):
        @pl.when(info[0] > 0)
        def _():
            kcopy = pltpu.make_async_copy(sk, mix, sem)
            kcopy.start()
            new[...] = jnp.dot(hid[...], w[:, D : 2 * D], preferred_element_type=f32).astype(bf16)
            kcopy.wait()
            settle(info, new, mix)
            turn(mix, 0, D, turned)

    (keys_turned,) = call(
        third,
        [near(D, N, f32)],
        [VM],
        [info, hidden, late_weight, far(stale_keys)],
        [SM, VM, VM, ANY],
        [vm((R, D), bf16), vm((N, D), bf16), DMA],
    )
    keys_turned = here(keys_turned)

    own, told = [], []
    kt = vt = vnew = vall = held = out = None
    project_at, turn_at = 1, 2

    for c, qs in enumerate(chunks):
        s = c + LAG
        after = chunks[s] if s < len(chunks) else ()
        group = groups[c - turn_at] if c >= turn_at else ()

        def reply(info, xr, ktf, vtf, stash, *rest, c=c, qs=qs, after=after, group=group):
            if c == project_at:
                hid, w, sv, so, x, vnew, vall, held, sems = rest
            elif c == turn_at:
                gains, keys_turned, qx, *sent, vnew, vall, held, x, terms, kt, vt, out, mix, turned, sem = rest
            elif group:
                kt, vt, qx, *sent, x, terms = rest
            else:
                (x,) = rest

            @pl.when(info[0] == 0)
            def _():
                answer(xr, ktf, vtf, qs, x)

            @pl.when(info[0] > 0)
            def _():
                if after:
                    at = QR * (after[0] - chunks[LAG][0])
                    x[0 : QR * len(after), :] = stash[at : at + QR * len(after), :]
                if c == project_at:
                    vcopy = pltpu.make_async_copy(sv, vall, sems.at[0])
                    vcopy.start()
                    ocopy = pltpu.make_async_copy(so, held, sems.at[1])
                    ocopy.start()
                    vnew[...] = jnp.dot(hid[...], w[:, 2 * D :], preferred_element_type=f32).astype(bf16)
                    vcopy.wait()
                    ocopy.wait()
                if c == turn_at:
                    ocopy = pltpu.make_async_copy(held, out, sem)
                    ocopy.start()
                    gain = gains[HD : 2 * HD, :]
                    for h in range(heads):
                        part = normed(keys_turned[HD * h : HD * (h + 1), :], gain)
                        kt[HP * h : HP * (h + 1), :] = padded(part, 0.0)
                    mix[...] = vall[...]
                    settle(info, vnew, mix)
                    turn(mix, 0, D, turned)
                    for h in range(heads):
                        vt[HP * h : HP * (h + 1), :] = padded(turned[HD * h : HD * (h + 1), :], 1.0)
                for i, h in enumerate(group):
                    q = own_query(h, sent, stash, qx)
                    terms[HP * i : HP * (i + 1), :] = score(q, head_of(kt, h), head_of(vt, h))
                if c == turn_at:
                    ocopy.wait()

        ins = [info, here(got[c]), kt_far, vt_far, stash]
        outs = [near(step_rows(s), LANES, bf16)]
        given = [VM] * len(ins[1:])
        spaces = [VM]
        scratch = []
        if c == project_at:
            ins += [hidden, late_weight, far(stale_values), far(stale_output)]
            given += [VM] * 2 + [ANY] * 2
            outs += [near(R, D, bf16), near(N, D, bf16), near(N, D, bf16)]
            spaces += [VM] * 3
            scratch = [DMA((2,))]
        elif c == turn_at:
            ins += [gains, keys_turned, qx, *sent, vnew, vall, held]
            given += [VM] * (6 + len(sent))
            outs += [near(HP * len(group), R, f32)] + [near(HP * heads, N, bf16)] * 2
            outs += [jax.ShapeDtypeStruct((N, D), bf16)]
            spaces += [VM] * 3 + [ANY]
            scratch = [vm((N, D), bf16), vm((D, N), f32), DMA]
        elif group:
            ins += [kt, vt, qx, *sent]
            given += [VM] * (3 + len(sent))
            outs += [near(HP * len(group), R, f32)]
            spaces += [VM]
        res = call(reply, outs, spaces, ins, [SM] + given, scratch)
        send(res[0])
        told.append(here(got[-1]))
        if c == project_at:
            vnew, vall, held = map(here, res[1:])
        elif group:
            own.append(here(res[1]))
            if c == turn_at:
                kt, vt, out = here(res[2]), here(res[3]), res[4]

    answers = chunks

    open_low = [HD * qs[0] // LANES * LANES for qs in answers]
    open_high = ceil_to(HD * (answers[-1][-1] + 1), LANES)

    def flush(info, turned, at, rows, out, ranges, sems):
        for low, high in ranges:
            for j in range(low, high, LANES):
                turn_back(turned, at, rows, j)
        for k, (low, high) in enumerate(ranges):
            write_rows(info, rows, out, low, high, sems.at[k])

    def settle_rows(rows, out, ranges, sems):
        for k, (low, high) in enumerate(ranges):
            wait_rows(rows, out, low, high, sems.at[k])

    def rest_of(info, so, kt, vt, qx, stash, *rest):
        sent, rest = rest[:LAG], rest[LAG:]
        kvs, rest = rest[:LAG], rest[LAG:]
        theirs, rest = rest[: len(answers) - 2], rest[len(answers) - 2 :]
        early, rest = rest[: len(groups) - 1], rest[len(groups) - 1 :]
        _, terms, keep, out, turned, rows, held, sems = rest
        own = (*early, terms)
        low = open_low[-2]

        @pl.when(info[0] == 0)
        def _():
            icopy = pltpu.make_async_copy(so, held, sems.at[0])
            ocopy = pltpu.make_async_copy(held, out, sems.at[1])
            icopy.start()
            icopy.wait()
            ocopy.start()
            ocopy.wait()

        @pl.when(info[0] > 0)
        def _():
            for i, h in enumerate(groups[-1]):
                q = own_query(h, sent, stash, qx)
                terms[HP * i : HP * (i + 1), :] = score(q, head_of(kt, h), head_of(vt, h))
            for i, h in enumerate(shipped):
                block = kvs[i][...].astype(f32)
                value = own_terms(own, h) + score(
                    qx[HP * i : HP * (i + 1), :],
                    padded(widen(block, 0, KB), 0.0),
                    padded(widen(block, KB, KB), 1.0),
                )
                turned[HD * h : HD * (h + 1), :] = value[:HD] / value[HD : HD + 1]
            for x, qs in zip(theirs, answers):
                merge(lambda h: own_terms(own, h), x, qs, turned, 0)
            ranges = [(0, low), (open_high, D)]
            flush(info, turned, 0, rows, out, ranges, sems)
            keep[...] = turned[low:open_high, :]
            settle_rows(rows, out, ranges, sems)

    ins = [
        info, far(stale_output), kt, vt, qx, stash, *sent,
        *map(here, got[:LAG]), *told[:-2], *own, out,
    ]
    terms, keep, out = call(
        rest_of,
        [
            near(HP * len(groups[-1]), R, f32),
            near(open_high - open_low[-2], R, f32),
            jax.ShapeDtypeStruct((N, D), bf16),
        ],
        [VM, VM, ANY],
        ins,
        [SM, ANY] + [VM] * (len(ins) - 3) + [ANY],
        [vm((D, R), f32), vm((R, D), bf16), vm((N, D), bf16), DMA((2,))],
        {len(ins) - 1: 2},
    )
    own.append(here(terms))

    def last(info, keep, theirs, latest, *rest):
        own, (_, out, turned, rows, sems) = rest[: len(groups)], rest[len(groups) :]
        low = open_low[-2]

        @pl.when(info[0] > 0)
        def _():
            turned[...] = keep[...]
            merge(lambda h: own_terms(own, h), theirs, answers[-2], turned, low)
            merge(lambda h: own_terms(own, h), latest, answers[-1], turned, low)
            flush(info, turned, low, rows, out, [(low, open_high)], sems)
            settle_rows(rows, out, [(low, open_high)], sems)

    return call(
        last,
        [jax.ShapeDtypeStruct((N, D), bf16)],
        [ANY],
        [info, here(keep), *told[-2:], *own, out],
        [SM, VM, VM, VM] + [VM] * len(own) + [ANY],
        [vm((open_high - open_low[-2], R), f32), vm((R, D), bf16), DMA((1,))],
        {4 + len(own): 0},
    )[0]


def pick_plan(mesh, token_count, model_width):
    patch = mesh.shape["patch"]
    own_rows = token_count // (mesh.shape["grp"] * patch)
    own_tiles = own_rows // TILE
    fresh_tiles = own_tiles * patch // 3
    if patch != 2 or fresh_tiles > own_tiles:
        return None
    return pair_plan(H, model_width, own_rows, fresh_tiles * TILE)


def solution(mesh):
    in_specs = (
        P(("grp", "patch"), None),
        P(),
        P(),
        P(),
        P(),
        P(),
        P(("grp", "patch"), None),
        P(("grp", "patch"), None),
        P(("grp", "patch"), None),
        P("grp"),
    )
    out_specs = P(("grp", "patch"), None)

    def whole(*arrays):
        plan = pick_plan(mesh, *arrays[0].shape)
        if plan is None:
            inner = body
        else:

            def inner(*blocks):
                return pair_body(plan, *blocks)

        step = jax.shard_map(
            inner, mesh=mesh, in_specs=in_specs, out_specs=out_specs, check_vma=False
        )
        return step(*arrays)

    return whole
```
